256 devices in a mesh: sub: 128 (over x_lo, y, z, core), row: 2 (over x_hi).
Axes of the slice: x: 4 (x_hi: 2, x_lo: 2; x = x_hi * 2 + x_lo), y: 4, z: 8, core: 2. Of those that a mesh axis runs over, the one named last changes fastest.
Arguments:
- compliance: bfloat16 [128, 36, 18, 128, 128], P('sub', 'row'), may hold values from -0.0625 to 0.0625
- block_columns: int32 [128, 36, 18], P('sub', 'row'), may hold values from 0 to 35, as said below
- load_response: bfloat16 [128, 32, 4608], P('sub', None, 'row'), may hold values from -6 to 6
- starting_motion: bfloat16 [128, 32, 4608], P('sub', None, 'row'), may hold values from -6 to 6
- start_traction: bfloat16 [128, 32, 4608], P('sub', None, 'row'), may hold values from -6 to 6
- stiffness: float32 [128, 4608], P('sub', 'row'), may hold values from 1 to 10
- history: float32 [128, 4608], P('sub', 'row'), may hold values from 0 to 0.6
- face_partner: int32 [128, 36], P('sub', 'row'), may hold values from -1 to 8, as said below
- orientation: int32 [128, 36, 128], P('sub', 'row'), may hold values from 0 to 127, as said below
Outputs:
- displacement: bfloat16 [128, 32, 4608], P('sub', None, 'row')
- traction: bfloat16 [128, 32, 4608], P('sub', None, 'row')
The draws below stay inside these ranges and needn't reach their ends.
Inputs may be any that keep to these rules, and one draw needn't show every extreme that they name: `block_columns`: each block row names 18 distinct face columns. `face_partner`: an entry is -1 for a free face, else the position, within the facing group of the same run of the neighbouring substructure, of the matched face. Matches are mutual. Faces facing s+1 on the last substructure and faces facing s-1 on the first are free. In some run of some substructure all 9 faces facing s+1 are matched. `orientation`: each face's row is a permutation of 0 to 127; matched faces carry mutually inverse permutations.
All inputs are finite; a program needn't handle non-finite values.
Results may differ from the reference program's by a relative error of at most 0.0045.
The reference program's roundings to bfloat16 on the way count: a program that leaves them out, or rounds other values in their place, can miss the bound.
Values may be sent and summed in bfloat16 or wider, within the bound.
A program may use at most 64 MiB of HBM per device.

```python
import math
import jax
import jax.numpy as jnp
from jax import lax

ORDER = 4608
SURFACE_EXTENT = 128
NNZB = 18
TIMES = 32
ITERS = 3
SUBS = 128
FACES = 36
GROUP = 9
N_ROW = 2


def shuffled(subkey, length):
    return jax.random.permutation(subkey, length).astype(jnp.int32)


def matching(key):
    halves = FACES // (2 * GROUP)
    keys = jax.random.split(key, 6)
    pairs = SUBS * halves
    choose = jax.random.randint(keys[0], (SUBS, halves), 0, 4)
    sparse = jax.random.randint(keys[1], (SUBS, halves), 0, GROUP // 3 + 1)
    counts = jnp.where(choose == 0, GROUP, sparse)
    busiest = jax.random.randint(keys[2], (), 0, max(SUBS - 1, 1))
    sub_ids = jnp.arange(SUBS)[:, None]
    counts = jnp.where(sub_ids == busiest, GROUP, counts)
    counts = jnp.where(sub_ids == SUBS - 1, 0, counts)
    perm_top = jax.vmap(lambda subkey: shuffled(subkey, GROUP))(jax.random.split(keys[3], pairs)).reshape(SUBS, halves, GROUP)
    perm_bottom = jax.vmap(lambda subkey: shuffled(subkey, GROUP))(jax.random.split(keys[4], pairs)).reshape(SUBS, halves, GROUP)
    inverse_top = jnp.argsort(perm_top, axis=-1).astype(jnp.int32)
    inverse_bottom = jnp.argsort(perm_bottom, axis=-1).astype(jnp.int32)
    top_entry = jnp.where(inverse_top < counts[..., None], jnp.take_along_axis(perm_bottom, inverse_top, axis=-1), -1)
    bottom_next = jnp.where(inverse_bottom < counts[..., None], jnp.take_along_axis(perm_top, inverse_bottom, axis=-1), -1)
    bottom_entry = jnp.concatenate([jnp.full((1, halves, GROUP), -1, jnp.int32), bottom_next[:-1]], axis=0)
    partner_table = jnp.concatenate([top_entry, bottom_entry], axis=2).reshape(SUBS, FACES)
    turns = jax.vmap(lambda subkey: shuffled(subkey, SURFACE_EXTENT))(jax.random.split(keys[5], pairs * GROUP)).reshape(SUBS, halves, GROUP, SURFACE_EXTENT)
    top_turn = jnp.take_along_axis(turns, jnp.broadcast_to(inverse_top[..., None], turns.shape), axis=2)
    bottom_pair = jnp.take_along_axis(turns, jnp.broadcast_to(inverse_bottom[..., None], turns.shape), axis=2)
    bottom_next_turn = jnp.argsort(bottom_pair, axis=-1).astype(jnp.int32)
    bottom_turn = jnp.concatenate([turns[:1], bottom_next_turn[:-1]], axis=0)
    turning = jnp.concatenate([top_turn, bottom_turn], axis=2).reshape(SUBS, FACES, SURFACE_EXTENT)
    return (partner_table.astype(jnp.int32), turning.astype(jnp.int32))


def draw_face_partner(key, part):
    return matching(jax.random.fold_in(key, 11))[0]


def draw_orientation(key, part):
    return matching(jax.random.fold_in(key, 11))[1]


def draw_block_columns(key, part):
    keys = jax.random.split(jax.random.fold_in(key, 5), SUBS * FACES)
    picked = jax.vmap(lambda subkey: shuffled(subkey, FACES)[:NNZB])(keys)
    return picked.reshape(SUBS, FACES, NNZB).astype(jnp.int32)


def levels(key, shape, pieces, least, largest):
    def one(dim, parts):
        steps = jax.random.uniform(jax.random.fold_in(jax.random.fold_in(key, 6), dim), (parts,), jnp.float32, least / len(pieces), largest / len(pieces))
        return jnp.repeat(jnp.exp(steps), shape[dim] // parts).reshape((-1,) + (1,) * (len(shape) - dim - 1))

    gain = one(*pieces[0])
    for cut in pieces[1:]:
        gain = gain * one(*cut)
    return gain


def bell_draw(rng, dims, spread, most, shards=(), kind=jnp.bfloat16):
    array = spread * jax.random.normal(rng, dims, jnp.float32)
    if shards:
        array = array * levels(rng, dims, shards, -0.22, 0.18)
    return jnp.clip(array, -most, most).astype(kind)


def setup_inputs(seed: int = 0) -> dict:
    arg_keys = jax.random.split(jax.random.key(seed), 10)
    return {
        "compliance": bell_draw(arg_keys[0], (SUBS, FACES, NNZB, SURFACE_EXTENT, SURFACE_EXTENT), (4 * SURFACE_EXTENT * NNZB) ** -0.5, 0.0625, ((0, 128), (1, 2))),
        "block_columns": draw_block_columns(jax.random.fold_in(arg_keys[9], 71), 0),
        "load_response": bell_draw(arg_keys[2], (SUBS, TIMES, ORDER), 1.0, 6.0, ((0, 128), (2, 2))),
        "starting_motion": bell_draw(arg_keys[3], (SUBS, TIMES, ORDER), 1.0, 6.0, ((0, 128), (2, 2))),
        "start_traction": bell_draw(arg_keys[4], (SUBS, TIMES, ORDER), 1.0, 6.0, ((0, 128), (2, 2))),
        "stiffness": jnp.clip(jnp.exp(math.log(10.0) - 2.3025851 * jax.random.uniform(arg_keys[5], (SUBS, ORDER), jnp.float32) ** levels(arg_keys[5], (SUBS, ORDER), ((0, 128), (1, 2)), -0.2, 0.2)), 1.0, 10.0),
        "history": jnp.clip(0.6 * jax.random.uniform(arg_keys[6], (SUBS, ORDER), jnp.float32) ** levels(arg_keys[6], (SUBS, ORDER), ((0, 128), (1, 2)), -0.2, 0.2), 0.0, 0.6),
        "face_partner": draw_face_partner(jax.random.fold_in(arg_keys[9], 71), 0),
        "orientation": draw_orientation(jax.random.fold_in(arg_keys[9], 71), 0),
    }


search_stiffness = 1.0
onset_jump = 0.15
failure_jump = 1.5


def cohesive(upward_marker, constitutive_parameters, opposing_surface, live_mask):
    temporal_points = upward_marker.shape[0]
    mate_upward_marker = opposing_surface[:temporal_points]
    joint_rigidity = 0.5 * (constitutive_parameters[0] + opposing_surface[temporal_points])
    joint_record = jnp.maximum(constitutive_parameters[1], opposing_surface[temporal_points + 1])
    difference = upward_marker - mate_upward_marker
    jump_size = difference / (search_stiffness + 2.0 * joint_rigidity)
    peak_jump = jnp.maximum(joint_record, lax.cummax(jnp.abs(jump_size), axis=0))
    damage = jnp.clip((peak_jump - onset_jump) / (failure_jump - onset_jump), 0.0, 1.0)
    effective = joint_rigidity * (1.0 - damage)
    traction = jnp.where(live_mask, effective * difference / (search_stiffness + 2.0 * effective), 0.0)
    displacement = (traction - upward_marker) / search_stiffness
    return displacement, traction


def reference(compliance, block_columns, load_response, starting_motion, start_traction, stiffness, history, face_partner, orientation):
    constitutive_parameters = jnp.stack([stiffness, history], axis=1).reshape(SUBS, 2, FACES, SURFACE_EXTENT)
    face_ids = jnp.arange(FACES, dtype=jnp.int32)
    within = face_ids % (FACES // N_ROW)
    run_start = face_ids - within
    facing_up = within < GROUP
    present_motion = starting_motion.astype(jnp.float32)
    present_stress = start_traction.astype(jnp.float32)

    def linear_section(operands):
        compliance_sub, columns, load_sub, disp_sub, trac_sub = operands
        robin_sum = trac_sub + search_stiffness * disp_sub
        flexibility_tiles = robin_sum.astype(jnp.bfloat16).reshape(TIMES, FACES, SURFACE_EXTENT)
        picked = jnp.take(flexibility_tiles, columns.astype(jnp.int32), axis=1).astype(jnp.float32)
        operator_multiply = jnp.einsum("tijb,ijab->tia", picked, compliance_sub.astype(jnp.float32))
        proportional_reaction = operator_multiply.reshape(TIMES, ORDER) + load_sub.astype(jnp.float32)
        return robin_sum - 2.0 * search_stiffness * proportional_reaction

    for iteration in range(ITERS):
        ascent_all = lax.map(linear_section, (compliance, block_columns, load_response, present_motion, present_stress))
        payload_all = jnp.concatenate([ascent_all.reshape(SUBS, TIMES, FACES, SURFACE_EXTENT), constitutive_parameters], axis=1)

        def local_section(sub_index):
            upper_payload = lax.dynamic_index_in_dim(payload_all, jnp.minimum(sub_index + 1, SUBS - 1), 0, keepdims=False)
            lower_payload = lax.dynamic_index_in_dim(payload_all, jnp.maximum(sub_index - 1, 0), 0, keepdims=False)
            own_payload = lax.dynamic_index_in_dim(payload_all, sub_index, 0, keepdims=False)
            partner_table = lax.dynamic_index_in_dim(face_partner, sub_index, 0, keepdims=False)
            turning = lax.dynamic_index_in_dim(orientation, sub_index, 0, keepdims=False)
            live_mask = (partner_table >= 0)[:, None]
            safe_index = jnp.maximum(partner_table, 0)
            source = jnp.where(facing_up, run_start + GROUP + safe_index, run_start + safe_index).astype(jnp.int32)
            chosen = jnp.where(facing_up[None, :, None], jnp.take(upper_payload, source, axis=1), jnp.take(lower_payload, source, axis=1))
            opposing_surface = jnp.take_along_axis(chosen, jnp.broadcast_to(turning[None], chosen.shape).astype(jnp.int32), axis=2)
            motion_distribution, stress_distribution = cohesive(own_payload[:TIMES], own_payload[TIMES:], opposing_surface, live_mask)
            return motion_distribution.reshape(TIMES, ORDER), stress_distribution.reshape(TIMES, ORDER)

        present_motion, present_stress = lax.map(local_section, jnp.arange(SUBS, dtype=jnp.int32))
    return present_motion.astype(jnp.bfloat16), present_stress.astype(jnp.bfloat16)
```

```python
import functools

import jax
import jax.numpy as jnp
from jax import lax
from jax.experimental import pallas as pl
from jax.experimental.pallas import tpu as pltpu
from jax.sharding import PartitionSpec as P

EXTENT = 128
ITERS = 3
ONSET = 0.15
FAILURE = 1.5
MESH = pl.DeviceIdType.MESH


def running_max(values):
    times = values.shape[0]
    step = 1
    while step < times:
        fill = jnp.zeros((step, values.shape[1]), values.dtype)
        values = jnp.maximum(values, jnp.concatenate([fill, values[: times - step]], axis=0))
        step *= 2
    return values


def kernel(
    columns,
    partners,
    compliance_hbm,
    load_hbm,
    motion_hbm,
    traction_hbm,
    stiffness,
    history,
    orientation,
    motion_out,
    traction_out,
    *scratch,
):
    (compliance, load, motion, traction, robin, own_law, law_below, law_above, pair_law) = scratch[:9]
    halves = scratch[9:12]
    ascents = scratch[12:15]
    belows = scratch[15:18]
    aboves = scratch[18:21]
    (block_sem, input_sem, law_send, law_recv, row_send, row_recv, up_send, down_send, below_recv, above_recv) = scratch[21:]

    faces = compliance.shape[0]
    stored = compliance.shape[1]
    times = motion.shape[0]
    group = faces // 2
    sub = lax.axis_index("sub")
    row = lax.axis_index("row")
    last = lax.axis_size("sub") - 1
    has_below = sub > 0
    has_above = sub < last
    below = jnp.maximum(sub - 1, 0)
    above = jnp.minimum(sub + 1, last)

    def lanes(face):
        if isinstance(face, int):
            return pl.ds(face * EXTENT, EXTENT)
        return pl.ds(pl.multiple_of(face * EXTENT, EXTENT), EXTENT)

    motion_copy = pltpu.make_async_copy(motion_hbm, motion, input_sem.at[0])
    traction_copy = pltpu.make_async_copy(traction_hbm, traction, input_sem.at[1])
    load_copy = pltpu.make_async_copy(load_hbm, load, input_sem.at[2])
    motion_copy.start()
    traction_copy.start()

    barrier = pltpu.get_barrier_semaphore()
    pl.semaphore_signal(barrier, inc=1, device_id={"row": 1 - row}, device_id_type=MESH)

    @pl.when(has_below)
    def _():
        pl.semaphore_signal(barrier, inc=1, device_id={"sub": below}, device_id_type=MESH)

    @pl.when(has_above)
    def _():
        pl.semaphore_signal(barrier, inc=1, device_id={"sub": above}, device_id_type=MESH)

    def block_copy(face):
        return pltpu.make_async_copy(compliance_hbm.at[face], compliance.at[face], block_sem.at[face])

    for face in range(faces):
        block_copy(face).start()
    load_copy.start()

    for face in range(faces):
        own_law[face, 0:4] = jnp.broadcast_to(stiffness[0:1, lanes(face)], (4, EXTENT))
        own_law[face, 4:8] = jnp.broadcast_to(history[0:1, lanes(face)], (4, EXTENT))

    base = row * faces

    def send_half(iteration, face):
        return pltpu.make_async_remote_copy(
            src_ref=halves[iteration].at[base + face],
            dst_ref=halves[iteration].at[base + face],
            send_sem=row_send.at[iteration],
            recv_sem=row_recv.at[iteration],
            device_id={"row": 1 - row},
            device_id_type=MESH,
        )

    def all_halves(iteration):
        return pltpu.make_async_remote_copy(
            src_ref=halves[iteration].at[pl.ds(base, faces)],
            dst_ref=halves[iteration].at[pl.ds(base, faces)],
            send_sem=row_send.at[iteration],
            recv_sem=row_recv.at[iteration],
            device_id={"row": 1 - row},
            device_id_type=MESH,
        )

    motion_copy.wait()
    traction_copy.wait()
    for face in range(faces):
        total = traction[:, lanes(face)].astype(jnp.float32) + motion[:, lanes(face)].astype(jnp.float32)
        robin[face] = total
        halves[0][base + face] = total.astype(jnp.bfloat16)

    pl.semaphore_wait(barrier, 1 + has_below.astype(jnp.int32) + has_above.astype(jnp.int32))

    all_halves(0).start()

    def law_up():
        return pltpu.make_async_remote_copy(
            src_ref=own_law.at[pl.ds(0, group)],
            dst_ref=law_below,
            send_sem=law_send.at[0],
            recv_sem=law_recv.at[0],
            device_id={"sub": above},
            device_id_type=MESH,
        )

    def law_down():
        return pltpu.make_async_remote_copy(
            src_ref=own_law.at[pl.ds(group, group)],
            dst_ref=law_above,
            send_sem=law_send.at[1],
            recv_sem=law_recv.at[1],
            device_id={"sub": below},
            device_id_type=MESH,
        )

    def up(iteration, start, count):
        return pltpu.make_async_remote_copy(
            src_ref=ascents[iteration].at[pl.ds(start, count)],
            dst_ref=belows[iteration].at[pl.ds(start, count)],
            send_sem=up_send.at[iteration],
            recv_sem=below_recv.at[iteration],
            device_id={"sub": above},
            device_id_type=MESH,
        )

    def down(iteration, start, count):
        return pltpu.make_async_remote_copy(
            src_ref=ascents[iteration].at[pl.ds(group + start, count)],
            dst_ref=aboves[iteration].at[pl.ds(start, count)],
            send_sem=down_send.at[iteration],
            recv_sem=above_recv.at[iteration],
            device_id={"sub": below},
            device_id_type=MESH,
        )

    @pl.when(has_above)
    def _():
        law_up().start()

    @pl.when(has_below)
    def _():
        law_down().start()

    load_copy.wait()

    for iteration in range(ITERS):
        half = halves[iteration]
        ascent_buffer = ascents[iteration]
        all_halves(iteration).wait_recv()

        def linear(face):
            if iteration == 0:
                block_copy(face).wait()
            total = None
            for pair in range(stored // 2):
                left = half[columns[0, face, 2 * pair]]
                right = half[columns[0, face, 2 * pair + 1]]
                piece = jnp.concatenate([left, right], axis=1)
                block = jnp.concatenate([compliance[face, 2 * pair], compliance[face, 2 * pair + 1]], axis=1)
                product = lax.dot_general(
                    piece, block, (((1,), (1,)), ((), ())), preferred_element_type=jnp.float32
                )
                total = product if total is None else total + product
            response = load[:, lanes(face)].astype(jnp.float32) + total
            ascent_buffer[face] = robin[face] - 2.0 * response

        def linear_up(face, carry):
            linear(face)

            @pl.when(has_above)
            def _():
                up(iteration, face, 1).start()

            return carry

        def linear_down(face, carry):
            linear(group + face)

            @pl.when(has_below)
            def _():
                down(iteration, face, 1).start()

            return carry

        lax.fori_loop(0, group, linear_up, 0)
        lax.fori_loop(0, group, linear_down, 0)

        def local(face, mates, mate_laws):
            partner = partners[0, face]
            index = jnp.maximum(partner, 0)
            turn = orientation[pl.ds(face, 1)]
            if iteration == 0:
                mate_law = jnp.take_along_axis(
                    mate_laws[index], jnp.broadcast_to(turn, (8, EXTENT)), axis=1
                )
                law = own_law[face]
                rigidity = 0.5 * (law[0:4] + mate_law[0:4])
                record = jnp.maximum(law[4:8], mate_law[4:8])
                pair_law[face, 0:4] = rigidity
                pair_law[face, 4:8] = record
            else:
                law = pair_law[face]
                rigidity = law[0:4]
                record = law[4:8]
            rigidity = rigidity[0:1]
            record = record[0:1]
            mate = jnp.take_along_axis(mates[index], jnp.broadcast_to(turn, (times, EXTENT)), axis=1)
            ascent = ascent_buffer[face]
            difference = ascent - mate
            jump = difference * (1.0 / (1.0 + 2.0 * rigidity))
            peak = jnp.maximum(record, running_max(jnp.abs(jump)))
            damage = jnp.clip((peak - ONSET) * (1.0 / (FAILURE - ONSET)), 0.0, 1.0)
            effective = rigidity * (1.0 - damage)
            live = jnp.full((times, EXTENT), partner, jnp.int32) >= 0
            stress = jnp.where(live, effective * difference / (1.0 + 2.0 * effective), 0.0)
            shift = stress - ascent
            if iteration == ITERS - 1:
                motion_out[:, lanes(face)] = shift.astype(jnp.bfloat16)
                traction_out[:, lanes(face)] = stress.astype(jnp.bfloat16)
            else:
                total = stress + shift
                robin[face] = total
                halves[iteration + 1][base + face] = total.astype(jnp.bfloat16)
                send_half(iteration + 1, face).start()

        @pl.when(has_below)
        def _():
            if iteration == 0:
                law_up().wait_recv()
            up(iteration, 0, group).wait_recv()

        def local_down(face, carry):
            local(group + face, belows[iteration], law_below)
            return carry

        lax.fori_loop(0, group, local_down, 0)

        @pl.when(has_above)
        def _():
            if iteration == 0:
                law_down().wait_recv()
            down(iteration, 0, group).wait_recv()

        def local_up(face, carry):
            local(face, aboves[iteration], law_above)
            return carry

        lax.fori_loop(0, group, local_up, 0)

    for iteration in range(ITERS):
        all_halves(iteration).wait_send()

    @pl.when(has_above)
    def _():
        law_up().wait_send()
        for iteration in range(ITERS):
            up(iteration, 0, group).wait_send()

    @pl.when(has_below)
    def _():
        law_down().wait_send()
        for iteration in range(ITERS):
            down(iteration, 0, group).wait_send()


def shards(
    compliance,
    block_columns,
    load_response,
    starting_motion,
    start_traction,
    stiffness,
    history,
    face_partner,
    orientation,
):
    faces, stored = block_columns.shape[1:]
    times, width = starting_motion.shape[1:]
    group = faces // 2
    rows = lax.axis_size("row")
    smem = pl.BlockSpec(memory_space=pltpu.SMEM)
    vmem = pl.BlockSpec(memory_space=pltpu.VMEM)
    hbm = pl.BlockSpec(memory_space=pl.ANY)
    bf16 = jnp.bfloat16
    f32 = jnp.float32
    dma = pltpu.SemaphoreType.DMA
    scratch = (
        [
            pltpu.VMEM((faces, stored, EXTENT, EXTENT), bf16),
            pltpu.VMEM((times, width), bf16),
            pltpu.VMEM((times, width), bf16),
            pltpu.VMEM((times, width), bf16),
            pltpu.VMEM((faces, times, EXTENT), f32),
            pltpu.VMEM((faces, 8, EXTENT), f32),
            pltpu.VMEM((group, 8, EXTENT), f32),
            pltpu.VMEM((group, 8, EXTENT), f32),
            pltpu.VMEM((faces, 8, EXTENT), f32),
        ]
        + [pltpu.VMEM((rows * faces, times, EXTENT), bf16)] * ITERS
        + [pltpu.VMEM((faces, times, EXTENT), f32)] * ITERS
        + [pltpu.VMEM((group, times, EXTENT), f32)] * (2 * ITERS)
        + [dma((faces,)), dma((3,)), dma((2,)), dma((2,))]
        + [dma((ITERS,))] * 6
    )
    motion, traction = pl.pallas_call(
        kernel,
        out_shape=[jax.ShapeDtypeStruct((times, width), bf16)] * 2,
        in_specs=[smem, smem, hbm, hbm, hbm, hbm, vmem, vmem, vmem],
        out_specs=[vmem, vmem],
        scratch_shapes=scratch,
        compiler_params=pltpu.CompilerParams(
            collective_id=0, has_side_effects=True, vmem_limit_bytes=40 << 20
        ),
        name="latin",
    )(
        block_columns,
        face_partner,
        compliance[0],
        load_response[0],
        starting_motion[0],
        start_traction[0],
        stiffness,
        history,
        orientation[0],
    )
    return motion[None], traction[None]


def solution(mesh):
    in_specs = (
        P("sub", "row", None, None, None),
        P("sub", "row", None),
        P("sub", None, "row"),
        P("sub", None, "row"),
        P("sub", None, "row"),
        P("sub", "row"),
        P("sub", "row"),
        P("sub", "row"),
        P("sub", "row", None),
    )
    out_specs = (P("sub", None, "row"), P("sub", None, "row"))
    return jax.shard_map(shards, mesh=mesh, in_specs=in_specs, out_specs=out_specs, check_vma=False)
```

```python
import functools

import jax
import jax.numpy as jnp
from jax import lax
from jax.experimental import pallas as pl
from jax.experimental.pallas import tpu as pltpu
from jax.sharding import PartitionSpec as P

EXTENT = 128
ITERS = 3
ONSET = 0.15
FAILURE = 1.5
MESH = pl.DeviceIdType.MESH


def running_max(values):
    times = values.shape[0]
    step = 1
    while step < times:
        fill = jnp.zeros((step, values.shape[1]), values.dtype)
        values = jnp.maximum(values, jnp.concatenate([fill, values[: times - step]], axis=0))
        step *= 2
    return values


def kernel(
    columns_hbm,
    partners_hbm,
    compliance_hbm,
    load_hbm,
    motion_hbm,
    traction_hbm,
    stiffness_hbm,
    history_hbm,
    orientation_hbm,
    motion_out,
    traction_out,
    *scratch,
):
    (compliance, load, motion, traction, robin, own_law, law_below, law_above, pair_law) = scratch[:9]
    columns, partners, stiffness, history, orientation = scratch[9:14]
    scratch = scratch[5:]
    halves = scratch[9:12]
    ascents = scratch[12:15]
    belows = scratch[15:18]
    aboves = scratch[18:21]
    (block_sem, input_sem, law_send, law_recv, row_send, row_recv, up_send, down_send, below_recv, above_recv) = scratch[21:]

    faces = compliance.shape[0]
    stored = compliance.shape[1]
    times = motion.shape[0]
    group = faces // 2
    sub = lax.axis_index("sub")
    row = lax.axis_index("row")
    last = lax.axis_size("sub") - 1
    has_below = sub > 0
    has_above = sub < last
    below = jnp.maximum(sub - 1, 0)
    above = jnp.minimum(sub + 1, last)

    def lanes(face):
        if isinstance(face, int):
            return pl.ds(face * EXTENT, EXTENT)
        return pl.ds(pl.multiple_of(face * EXTENT, EXTENT), EXTENT)

    motion_copy = pltpu.make_async_copy(motion_hbm, motion, input_sem.at[0])
    traction_copy = pltpu.make_async_copy(traction_hbm, traction, input_sem.at[1])
    load_copy = pltpu.make_async_copy(load_hbm, load, input_sem.at[2])
    law_copies = [
        pltpu.make_async_copy(stiffness_hbm, stiffness, input_sem.at[3]),
        pltpu.make_async_copy(history_hbm, history, input_sem.at[4]),
    ]
    columns_copy = pltpu.make_async_copy(columns_hbm, columns, input_sem.at[5])
    match_copies = [
        pltpu.make_async_copy(partners_hbm, partners, input_sem.at[6]),
        pltpu.make_async_copy(orientation_hbm, orientation, input_sem.at[7]),
    ]
    motion_copy.start()
    traction_copy.start()
    for copy in law_copies:
        copy.start()
    columns_copy.start()

    barrier = pltpu.get_barrier_semaphore()
    pl.semaphore_signal(barrier, inc=1, device_id={"row": 1 - row}, device_id_type=MESH)

    @pl.when(has_below)
    def _():
        pl.semaphore_signal(barrier, inc=1, device_id={"sub": below}, device_id_type=MESH)

    @pl.when(has_above)
    def _():
        pl.semaphore_signal(barrier, inc=1, device_id={"sub": above}, device_id_type=MESH)

    def block_copy(face):
        return pltpu.make_async_copy(compliance_hbm.at[face], compliance.at[face], block_sem.at[face])

    for face in range(faces):
        block_copy(face).start()
    load_copy.start()
    for copy in match_copies:
        copy.start()

    base = row * faces

    def send_half(iteration, face):
        return pltpu.make_async_remote_copy(
            src_ref=halves[iteration].at[base + face],
            dst_ref=halves[iteration].at[base + face],
            send_sem=row_send.at[iteration],
            recv_sem=row_recv.at[iteration],
            device_id={"row": 1 - row},
            device_id_type=MESH,
        )

    def all_halves(iteration):
        return pltpu.make_async_remote_copy(
            src_ref=halves[iteration].at[pl.ds(base, faces)],
            dst_ref=halves[iteration].at[pl.ds(base, faces)],
            send_sem=row_send.at[iteration],
            recv_sem=row_recv.at[iteration],
            device_id={"row": 1 - row},
            device_id_type=MESH,
        )

    motion_copy.wait()
    traction_copy.wait()
    for face in range(faces):
        total = traction[:, lanes(face)].astype(jnp.float32) + motion[:, lanes(face)].astype(jnp.float32)
        robin[face] = total
        halves[0][base + face] = total.astype(jnp.bfloat16)

    pl.semaphore_wait(barrier, 1 + has_below.astype(jnp.int32) + has_above.astype(jnp.int32))

    all_halves(0).start()

    for copy in law_copies:
        copy.wait()
    for face in range(faces):
        own_law[face, 0:4] = jnp.broadcast_to(stiffness[0:1, lanes(face)], (4, EXTENT))
        own_law[face, 4:8] = jnp.broadcast_to(history[0:1, lanes(face)], (4, EXTENT))

    def law_up():
        return pltpu.make_async_remote_copy(
            src_ref=own_law.at[pl.ds(0, group)],
            dst_ref=law_below,
            send_sem=law_send.at[0],
            recv_sem=law_recv.at[0],
            device_id={"sub": above},
            device_id_type=MESH,
        )

    def law_down():
        return pltpu.make_async_remote_copy(
            src_ref=own_law.at[pl.ds(group, group)],
            dst_ref=law_above,
            send_sem=law_send.at[1],
            recv_sem=law_recv.at[1],
            device_id={"sub": below},
            device_id_type=MESH,
        )

    def up(iteration, start, count):
        return pltpu.make_async_remote_copy(
            src_ref=ascents[iteration].at[pl.ds(start, count)],
            dst_ref=belows[iteration].at[pl.ds(start, count)],
            send_sem=up_send.at[iteration],
            recv_sem=below_recv.at[iteration],
            device_id={"sub": above},
            device_id_type=MESH,
        )

    def down(iteration, start, count):
        return pltpu.make_async_remote_copy(
            src_ref=ascents[iteration].at[pl.ds(group + start, count)],
            dst_ref=aboves[iteration].at[pl.ds(start, count)],
            send_sem=down_send.at[iteration],
            recv_sem=above_recv.at[iteration],
            device_id={"sub": below},
            device_id_type=MESH,
        )

    @pl.when(has_above)
    def _():
        law_up().start()

    @pl.when(has_below)
    def _():
        law_down().start()

    load_copy.wait()
    columns_copy.wait()

    for iteration in range(ITERS):
        half = halves[iteration]
        ascent_buffer = ascents[iteration]
        all_halves(iteration).wait_recv()

        def linear(face):
            if iteration == 0:
                block_copy(face).wait()
            total = None
            for pair in range(stored // 2):
                left = half[columns[face, 0, 2 * pair]]
                right = half[columns[face, 0, 2 * pair + 1]]
                piece = jnp.concatenate([left, right], axis=1)
                block = jnp.concatenate([compliance[face, 2 * pair], compliance[face, 2 * pair + 1]], axis=1)
                product = lax.dot_general(
                    piece, block, (((1,), (1,)), ((), ())), preferred_element_type=jnp.float32
                )
                total = product if total is None else total + product
            response = load[:, lanes(face)].astype(jnp.float32) + total
            ascent_buffer[face] = robin[face] - 2.0 * response

        def linear_up(face, carry):
            linear(face)

            @pl.when(has_above)
            def _():
                up(iteration, face, 1).start()

            return carry

        def linear_down(face, carry):
            linear(group + face)

            @pl.when(has_below)
            def _():
                down(iteration, face, 1).start()

            return carry

        lax.fori_loop(0, group, linear_up, 0)
        lax.fori_loop(0, group, linear_down, 0)

        def local(face, mates, mate_laws):
            partner = partners[0, face]
            index = jnp.maximum(partner, 0)
            turn = orientation[face]
            if iteration == 0:
                mate_law = jnp.take_along_axis(
                    mate_laws[index], jnp.broadcast_to(turn, (8, EXTENT)), axis=1
                )
                law = own_law[face]
                rigidity = 0.5 * (law[0:4] + mate_law[0:4])
                record = jnp.maximum(law[4:8], mate_law[4:8])
                pair_law[face, 0:4] = rigidity
                pair_law[face, 4:8] = record
            else:
                law = pair_law[face]
                rigidity = law[0:4]
                record = law[4:8]
            rigidity = rigidity[0:1]
            record = record[0:1]
            mate = jnp.take_along_axis(mates[index], jnp.broadcast_to(turn, (times, EXTENT)), axis=1)
            ascent = ascent_buffer[face]
            difference = ascent - mate
            jump = difference * (1.0 / (1.0 + 2.0 * rigidity))
            peak = jnp.maximum(record, running_max(jnp.abs(jump)))
            damage = jnp.clip((peak - ONSET) * (1.0 / (FAILURE - ONSET)), 0.0, 1.0)
            effective = rigidity * (1.0 - damage)
            live = jnp.full((times, EXTENT), partner, jnp.int32) >= 0
            stress = jnp.where(live, effective * difference / (1.0 + 2.0 * effective), 0.0)
            shift = stress - ascent
            if iteration == ITERS - 1:
                motion_out[:, lanes(face)] = shift.astype(jnp.bfloat16)
                traction_out[:, lanes(face)] = stress.astype(jnp.bfloat16)
            else:
                total = stress + shift
                robin[face] = total
                halves[iteration + 1][base + face] = total.astype(jnp.bfloat16)
                send_half(iteration + 1, face).start()

        if iteration == 0:
            for copy in match_copies:
                copy.wait()

        @pl.when(has_below)
        def _():
            if iteration == 0:
                law_up().wait_recv()
            up(iteration, 0, group).wait_recv()

        def local_down(face, carry):
            local(group + face, belows[iteration], law_below)
            return carry

        lax.fori_loop(0, group, local_down, 0)

        @pl.when(has_above)
        def _():
            if iteration == 0:
                law_down().wait_recv()
            down(iteration, 0, group).wait_recv()

        def local_up(face, carry):
            local(face, aboves[iteration], law_above)
            return carry

        lax.fori_loop(0, group, local_up, 0)

    for iteration in range(ITERS):
        all_halves(iteration).wait_send()

    @pl.when(has_above)
    def _():
        law_up().wait_send()
        for iteration in range(ITERS):
            up(iteration, 0, group).wait_send()

    @pl.when(has_below)
    def _():
        law_down().wait_send()
        for iteration in range(ITERS):
            down(iteration, 0, group).wait_send()


def shards(
    compliance,
    block_columns,
    load_response,
    starting_motion,
    start_traction,
    stiffness,
    history,
    face_partner,
    orientation,
):
    faces, stored = block_columns.shape[1:]
    times, width = starting_motion.shape[1:]
    group = faces // 2
    rows = lax.axis_size("row")
    vmem = pl.BlockSpec(memory_space=pltpu.VMEM)
    hbm = pl.BlockSpec(memory_space=pltpu.HBM)
    bf16 = jnp.bfloat16
    f32 = jnp.float32
    dma = pltpu.SemaphoreType.DMA
    scratch = (
        [
            pltpu.VMEM((faces, stored, EXTENT, EXTENT), bf16),
            pltpu.VMEM((times, width), bf16),
            pltpu.VMEM((times, width), bf16),
            pltpu.VMEM((times, width), bf16),
            pltpu.VMEM((faces, times, EXTENT), f32),
            pltpu.VMEM((faces, 8, EXTENT), f32),
            pltpu.VMEM((group, 8, EXTENT), f32),
            pltpu.VMEM((group, 8, EXTENT), f32),
            pltpu.VMEM((faces, 8, EXTENT), f32),
            pltpu.SMEM((faces, 1, stored), jnp.int32),
            pltpu.SMEM((1, faces), jnp.int32),
            pltpu.VMEM((1, width), f32),
            pltpu.VMEM((1, width), f32),
            pltpu.VMEM((faces, 1, EXTENT), jnp.int32),
        ]
        + [pltpu.VMEM((rows * faces, times, EXTENT), bf16)] * ITERS
        + [pltpu.VMEM((faces, times, EXTENT), f32)] * ITERS
        + [pltpu.VMEM((group, times, EXTENT), f32)] * (2 * ITERS)
        + [dma((faces,)), dma((8,)), dma((2,)), dma((2,))]
        + [dma((ITERS,))] * 6
    )
    motion, traction = pl.pallas_call(
        kernel,
        out_shape=[jax.ShapeDtypeStruct((times, width), bf16)] * 2,
        in_specs=[hbm] * 9,
        out_specs=[vmem, vmem],
        scratch_shapes=scratch,
        compiler_params=pltpu.CompilerParams(
            collective_id=0, has_side_effects=True, vmem_limit_bytes=67043328
        ),
        name="latin",
    )(
        jnp.transpose(block_columns, (1, 0, 2)),
        face_partner,
        compliance[0],
        load_response[0],
        starting_motion[0],
        start_traction[0],
        stiffness,
        history,
        jnp.transpose(orientation, (1, 0, 2)),
    )
    return motion[None], traction[None]


def solution(mesh):
    in_specs = (
        P("sub", "row", None, None, None),
        P("sub", "row", None),
        P("sub", None, "row"),
        P("sub", None, "row"),
        P("sub", None, "row"),
        P("sub", "row"),
        P("sub", "row"),
        P("sub", "row"),
        P("sub", "row", None),
    )
    out_specs = (P("sub", None, "row"), P("sub", None, "row"))
    return jax.shard_map(shards, mesh=mesh, in_specs=in_specs, out_specs=out_specs, check_vma=False)
```

```python
import jax
import jax.numpy as jnp
from jax import lax
from jax.experimental import pallas as pl
from jax.experimental.pallas import tpu as pltpu
from jax.sharding import PartitionSpec as P

EXTENT = 128
ITERS = 3
ONSET = 0.15
FAILURE = 1.5
SPAN = 1.0 / (FAILURE - ONSET)
CHUNK = 3
MESH = pl.DeviceIdType.MESH


def running_max(values):
    times = values.shape[0]
    step = 1
    while step < times:
        fill = jnp.zeros((step, values.shape[1]), values.dtype)
        values = jnp.maximum(values, jnp.concatenate([fill, values[: times - step]], axis=0))
        step *= 2
    return values


def kernel(
    columns_hbm,
    partners_hbm,
    compliance_hbm,
    load_hbm,
    motion_hbm,
    traction_hbm,
    stiffness_hbm,
    history_hbm,
    orientation_hbm,
    ascent_out,
    traction_out,
    compliance,
    load,
    motion,
    traction,
    columns,
    partners,
    stiffness,
    history,
    orientation,
    offset,
    own_law,
    near_law,
    far_law,
    pair_law,
    *scratch,
):
    halves = scratch[0:3]
    ascents = scratch[3:6]
    nears = scratch[6:9]
    fars = scratch[9:12]
    (block_sem, input_sem, law_send, law_recv, row_send, row_recv, near_send, near_recv, far_send, far_recv) = scratch[12:]

    faces, stored = compliance.shape[:2]
    times = motion.shape[0]
    group = faces // 2
    subs = lax.axis_size("sub")
    sub = lax.axis_index("sub")
    row = lax.axis_index("row")
    odd = lax.rem(sub, 2)
    near = {"sub": sub + 1 - 2 * odd}
    far = {"sub": lax.rem(sub + 2 * odd - 1 + subs, subs)}
    mirror = {"row": 1 - row}
    near_base = group * odd
    far_base = group * (1 - odd)
    base = row * faces

    def lanes(face):
        if isinstance(face, int):
            return pl.ds(face * EXTENT, EXTENT)
        return pl.ds(pl.multiple_of(face * EXTENT, EXTENT), EXTENT)

    def fetch(source, target, index):
        return pltpu.make_async_copy(source, target, input_sem.at[index])

    def block_copy(face):
        return pltpu.make_async_copy(compliance_hbm.at[face], compliance.at[face], block_sem.at[face])

    def push(source, target, send, recv, device):
        return pltpu.make_async_remote_copy(
            src_ref=source, dst_ref=target, send_sem=send, recv_sem=recv, device_id=device, device_id_type=MESH
        )

    motion_copy = fetch(motion_hbm, motion, 0)
    traction_copy = fetch(traction_hbm, traction, 1)
    stiffness_copy = fetch(stiffness_hbm, stiffness, 2)
    history_copy = fetch(history_hbm, history, 3)
    load_copy = fetch(load_hbm, load, 4)
    columns_copy = fetch(columns_hbm, columns, 5)
    partners_copy = fetch(partners_hbm, partners, 6)
    orientation_copy = fetch(orientation_hbm, orientation, 7)
    motion_copy.start()
    traction_copy.start()

    barrier = pltpu.get_barrier_semaphore()
    for device in (mirror, near, far):
        pl.semaphore_signal(barrier, inc=1, device_id=device, device_id_type=MESH)

    stiffness_copy.start()
    history_copy.start()
    load_copy.start()
    for face in range(faces):
        block_copy(face).start()
    for copy in (columns_copy, partners_copy, orientation_copy):
        copy.start()

    def send_half(iteration, start, count):
        part = halves[iteration].at[pl.ds(base + start, count)]
        return push(part, part, row_send.at[iteration], row_recv.at[iteration], mirror)

    def send_near(iteration, start, count):
        return push(
            ascents[iteration].at[pl.ds(near_base + start, count)],
            nears[iteration].at[pl.ds(start, count)],
            near_send.at[iteration],
            near_recv.at[iteration],
            near,
        )

    def send_far(iteration, start, count):
        return push(
            ascents[iteration].at[pl.ds(far_base + start, count)],
            fars[iteration].at[pl.ds(start, count)],
            far_send.at[iteration],
            far_recv.at[iteration],
            far,
        )

    near_law_copy = push(own_law.at[pl.ds(near_base, group)], near_law, law_send.at[0], law_recv.at[0], near)
    far_law_copy = push(own_law.at[pl.ds(far_base, group)], far_law, law_send.at[1], law_recv.at[1], far)

    motion_copy.wait()
    traction_copy.wait()
    for face in range(faces):
        total = traction[:, lanes(face)].astype(jnp.float32) + motion[:, lanes(face)].astype(jnp.float32)
        offset[face] = total
        halves[0][base + face] = total.astype(jnp.bfloat16)

    pl.semaphore_wait(barrier, 3)
    send_half(0, 0, faces).start()

    stiffness_copy.wait()
    history_copy.wait()
    for face in range(faces):
        own_law[face, 0:4] = jnp.broadcast_to(stiffness[0:1, lanes(face)], (4, EXTENT))
        own_law[face, 4:8] = jnp.broadcast_to(history[0:1, lanes(face)], (4, EXTENT))
    far_law_copy.start()
    near_law_copy.start()

    load_copy.wait()
    for face in range(faces):
        offset[face] = offset[face] - 2.0 * load[:, lanes(face)].astype(jnp.float32)

    def turn_blocks(face, carry):
        block_copy(face).wait()
        for slot in range(stored):
            compliance[face, slot] = compliance[face, slot].T
        return carry

    lax.fori_loop(0, faces, turn_blocks, 0)

    for copy in (columns_copy, partners_copy, orientation_copy):
        copy.wait()
    near_law_copy.wait_recv()
    far_law_copy.wait_recv()

    def join_laws(face, mate_laws):
        partner = partners[0, face]
        turn = jnp.broadcast_to(orientation[face], (8, EXTENT))
        mate = jnp.take_along_axis(mate_laws[jnp.maximum(partner, 0)], turn, axis=1)
        own = own_law[face]
        live = jnp.full((1, EXTENT), partner, jnp.int32) >= 0
        rigidity = jnp.where(live, 0.5 * (own[0:1] + mate[0:1]), 0.0)
        record = SPAN * jnp.maximum(own[4:5], mate[4:5])
        scale = SPAN / (1.0 + 2.0 * rigidity)
        pair_law[face, 0] = jnp.broadcast_to(rigidity, (8, EXTENT))
        pair_law[face, 1] = jnp.broadcast_to(record, (8, EXTENT))
        pair_law[face, 2] = jnp.broadcast_to(scale, (8, EXTENT))

    for index in range(group):
        join_laws(near_base + index, near_law)
    for index in range(group):
        join_laws(far_base + index, far_law)

    def tall(tile):
        return jnp.concatenate([tile] * (times // 8), axis=0)

    for iteration in range(ITERS):
        half = halves[iteration]
        ascent_buffer = ascents[iteration]
        send_half(iteration, 0, faces).wait_recv()

        def linear(face):
            total = None
            for pair in range(stored // 2):
                left = half[columns[face, 0, 2 * pair]]
                right = half[columns[face, 0, 2 * pair + 1]]
                piece = jnp.concatenate([left, right], axis=1)
                block = jnp.concatenate([compliance[face, 2 * pair], compliance[face, 2 * pair + 1]], axis=0)
                product = jnp.dot(piece, block, preferred_element_type=jnp.float32)
                total = product if total is None else total + product
            ascent_buffer[face] = offset[face] - 2.0 * total

        for start in range(0, group, CHUNK):
            for index in range(start, start + CHUNK):
                linear(far_base + index)
            send_far(iteration, start, CHUNK).start()
        for index in range(group):
            linear(near_base + index)
        send_near(iteration, 0, group).start()

        def local(face, mates):
            index = jnp.maximum(partners[0, face], 0)
            turn = jnp.broadcast_to(orientation[face], (times, EXTENT))
            rigidity = tall(pair_law[face, 0])
            record = tall(pair_law[face, 1])
            scale = tall(pair_law[face, 2])
            mate = jnp.take_along_axis(mates[index], turn, axis=1)
            ascent = ascent_buffer[face]
            difference = ascent - mate
            peak = jnp.maximum(record, running_max(jnp.abs(difference * scale)))
            effective = rigidity * jnp.clip(FAILURE * SPAN - peak, 0.0, 1.0)
            stress = effective * difference / (1.0 + 2.0 * effective)
            if iteration == ITERS - 1:
                ascent_out[:, lanes(face)] = ascent
                traction_out[:, lanes(face)] = stress
            else:
                total = stress + (stress - ascent)
                offset[face] = total - 2.0 * load[:, lanes(face)].astype(jnp.float32)
                halves[iteration + 1][base + face] = total.astype(jnp.bfloat16)

        send_near(iteration, 0, group).wait_recv()
        for start in range(0, group, CHUNK):
            for index in range(start, start + CHUNK):
                local(near_base + index, nears[iteration])
            if iteration < ITERS - 1:
                send_half(iteration + 1, near_base + start, CHUNK).start()
        send_far(iteration, 0, group).wait_recv()
        for start in range(0, group, CHUNK):
            for index in range(start, start + CHUNK):
                local(far_base + index, fars[iteration])
            if iteration < ITERS - 1:
                send_half(iteration + 1, far_base + start, CHUNK).start()

    near_law_copy.wait_send()
    far_law_copy.wait_send()
    for iteration in range(ITERS):
        send_half(iteration, 0, faces).wait_send()
        send_near(iteration, 0, group).wait_send()
        send_far(iteration, 0, group).wait_send()


def shards(
    compliance,
    block_columns,
    load_response,
    starting_motion,
    start_traction,
    stiffness,
    history,
    face_partner,
    orientation,
):
    faces, stored = block_columns.shape[1:]
    times, width = starting_motion.shape[1:]
    group = faces // 2
    rows = lax.axis_size("row")
    vmem = pl.BlockSpec(memory_space=pltpu.VMEM)
    hbm = pl.BlockSpec(memory_space=pltpu.HBM)
    bf16 = jnp.bfloat16
    f32 = jnp.float32
    dma = pltpu.SemaphoreType.DMA
    scratch = (
        [
            pltpu.VMEM((faces, stored, EXTENT, EXTENT), bf16),
            pltpu.VMEM((times, width), bf16),
            pltpu.VMEM((times, width), bf16),
            pltpu.VMEM((times, width), bf16),
            pltpu.SMEM((faces, 1, stored), jnp.int32),
            pltpu.SMEM((1, faces), jnp.int32),
            pltpu.VMEM((1, width), f32),
            pltpu.VMEM((1, width), f32),
            pltpu.VMEM((faces, 1, EXTENT), jnp.int32),
            pltpu.VMEM((faces, times, EXTENT), f32),
            pltpu.VMEM((faces, 8, EXTENT), f32),
            pltpu.VMEM((group, 8, EXTENT), f32),
            pltpu.VMEM((group, 8, EXTENT), f32),
            pltpu.VMEM((faces, 3, 8, EXTENT), f32),
        ]
        + [pltpu.VMEM((rows * faces, times, EXTENT), bf16)] * ITERS
        + [pltpu.VMEM((faces, times, EXTENT), f32)] * ITERS
        + [pltpu.VMEM((group, times, EXTENT), f32)] * (2 * ITERS)
        + [dma((faces,)), dma((8,)), dma((2,)), dma((2,))]
        + [dma((ITERS,))] * 6
    )
    ascent, traction = pl.pallas_call(
        kernel,
        out_shape=[jax.ShapeDtypeStruct((times, width), f32)] * 2,
        in_specs=[hbm] * 9,
        out_specs=[vmem, vmem],
        scratch_shapes=scratch,
        compiler_params=pltpu.CompilerParams(
            collective_id=0, has_side_effects=True, vmem_limit_bytes=67043328
        ),
        name="latin",
    )(
        jnp.transpose(block_columns, (1, 0, 2)),
        face_partner,
        compliance[0],
        load_response[0],
        starting_motion[0],
        start_traction[0],
        stiffness,
        history,
        jnp.transpose(orientation, (1, 0, 2)),
    )
    return (traction - ascent).astype(bf16)[None], traction.astype(bf16)[None]


def solution(mesh):
    in_specs = (
        P("sub", "row", None, None, None),
        P("sub", "row", None),
        P("sub", None, "row"),
        P("sub", None, "row"),
        P("sub", None, "row"),
        P("sub", "row"),
        P("sub", "row"),
        P("sub", "row"),
        P("sub", "row", None),
    )
    out_specs = (P("sub", None, "row"), P("sub", None, "row"))
    return jax.shard_map(shards, mesh=mesh, in_specs=in_specs, out_specs=out_specs, check_vma=False)
```

```python
import jax
import jax.numpy as jnp
from jax import lax
from jax.experimental import pallas as pl
from jax.experimental.pallas import tpu as pltpu
from jax.sharding import PartitionSpec as P

EXTENT = 128
ITERS = 3
ONSET = 0.15
FAILURE = 1.5
SPAN = 1.0 / (FAILURE - ONSET)
CHUNK = 3
MESH = pl.DeviceIdType.MESH


def running_max(values):
    times = values.shape[0]
    step = 1
    while step < times:
        fill = jnp.zeros((step, values.shape[1]), values.dtype)
        values = jnp.maximum(values, jnp.concatenate([fill, values[: times - step]], axis=0))
        step *= 2
    return values


def kernel(
    columns_hbm,
    partners_hbm,
    compliance_hbm,
    load_hbm,
    motion_hbm,
    traction_hbm,
    stiffness_hbm,
    history_hbm,
    orientation_hbm,
    ascent_out,
    traction_out,
    compliance,
    load,
    motion,
    traction,
    columns,
    partners,
    stiffness,
    history,
    orientation,
    offset,
    own_law,
    near_law,
    far_law,
    pair_law,
    *scratch,
):
    halves = scratch[0:3]
    ascents = scratch[3:6]
    nears = scratch[6:9]
    fars = scratch[9:12]
    (block_sem, input_sem, law_send, law_recv, row_send, row_recv, near_send, near_recv, far_send, far_recv) = scratch[12:]

    faces, stored = compliance.shape[:2]
    times = motion.shape[0]
    group = faces // 2
    subs = lax.axis_size("sub")
    sub = lax.axis_index("sub")
    row = lax.axis_index("row")
    odd = lax.rem(sub, 2)
    near = {"sub": sub + 1 - 2 * odd}
    far = {"sub": lax.rem(sub + 2 * odd - 1 + subs, subs)}
    mirror = {"row": 1 - row}
    near_base = group * odd
    far_base = group * (1 - odd)
    base = row * faces

    def lanes(face):
        if isinstance(face, int):
            return pl.ds(face * EXTENT, EXTENT)
        return pl.ds(pl.multiple_of(face * EXTENT, EXTENT), EXTENT)

    def fetch(source, target, index):
        return pltpu.make_async_copy(source, target, input_sem.at[index])

    def block_copy(face):
        return pltpu.make_async_copy(compliance_hbm.at[face], compliance.at[face], block_sem.at[face])

    def push(source, target, send, recv, device):
        return pltpu.make_async_remote_copy(
            src_ref=source, dst_ref=target, send_sem=send, recv_sem=recv, device_id=device, device_id_type=MESH
        )

    motion_copy = fetch(motion_hbm, motion, 0)
    traction_copy = fetch(traction_hbm, traction, 1)
    stiffness_copy = fetch(stiffness_hbm, stiffness, 2)
    history_copy = fetch(history_hbm, history, 3)
    load_copy = fetch(load_hbm, load, 4)
    columns_copy = fetch(columns_hbm, columns, 5)
    partners_copy = fetch(partners_hbm, partners, 6)
    orientation_copy = fetch(orientation_hbm, orientation, 7)
    motion_copy.start()
    traction_copy.start()

    barrier = pltpu.get_barrier_semaphore()
    for device in (mirror, near, far):
        pl.semaphore_signal(barrier, inc=1, device_id=device, device_id_type=MESH)

    stiffness_copy.start()
    history_copy.start()
    load_copy.start()
    for face in range(faces):
        block_copy(face).start()
    for copy in (columns_copy, partners_copy, orientation_copy):
        copy.start()

    def send_half(iteration, start, count):
        part = halves[iteration].at[pl.ds(base + start, count)]
        return push(part, part, row_send.at[iteration], row_recv.at[iteration], mirror)

    def send_near(iteration, start, count):
        return push(
            ascents[iteration].at[pl.ds(near_base + start, count)],
            nears[iteration].at[pl.ds(start, count)],
            near_send.at[iteration],
            near_recv.at[iteration],
            near,
        )

    def send_far(iteration, start, count):
        return push(
            ascents[iteration].at[pl.ds(far_base + start, count)],
            fars[iteration].at[pl.ds(start, count)],
            far_send.at[iteration],
            far_recv.at[iteration],
            far,
        )

    near_law_copy = push(own_law.at[pl.ds(near_base, group)], near_law, law_send.at[0], law_recv.at[0], near)
    far_law_copy = push(own_law.at[pl.ds(far_base, group)], far_law, law_send.at[1], law_recv.at[1], far)

    motion_copy.wait()
    traction_copy.wait()
    for face in range(faces):
        total = traction[:, lanes(face)].astype(jnp.float32) + motion[:, lanes(face)].astype(jnp.float32)
        offset[face] = total
        halves[0][base + face] = total.astype(jnp.bfloat16)

    pl.semaphore_wait(barrier, 3)
    send_half(0, 0, faces).start()

    stiffness_copy.wait()
    history_copy.wait()
    for face in range(faces):
        own_law[face, 0:4] = jnp.broadcast_to(stiffness[0:1, lanes(face)], (4, EXTENT))
        own_law[face, 4:8] = jnp.broadcast_to(history[0:1, lanes(face)], (4, EXTENT))
    far_law_copy.start()
    near_law_copy.start()

    load_copy.wait()
    for face in range(faces):
        offset[face] = offset[face] - 2.0 * load[:, lanes(face)].astype(jnp.float32)

    def turn_blocks(face, carry):
        block_copy(face).wait()
        for slot in range(stored):
            compliance[face, slot] = compliance[face, slot].T
        return carry

    lax.fori_loop(0, faces, turn_blocks, 0)

    for copy in (columns_copy, partners_copy, orientation_copy):
        copy.wait()
    near_law_copy.wait_recv()
    far_law_copy.wait_recv()

    def join_laws(face, mate_laws):
        partner = partners[0, face]
        turn = jnp.broadcast_to(orientation[face], (8, EXTENT))
        mate = jnp.take_along_axis(mate_laws[jnp.maximum(partner, 0)], turn, axis=1)
        own = own_law[face]
        live = jnp.full((1, EXTENT), partner, jnp.int32) >= 0
        rigidity = jnp.where(live, 0.5 * (own[0:1] + mate[0:1]), 0.0)
        record = SPAN * jnp.maximum(own[4:5], mate[4:5])
        scale = SPAN / (1.0 + 2.0 * rigidity)
        pair_law[face, 0] = jnp.broadcast_to(rigidity, (8, EXTENT))
        pair_law[face, 1] = jnp.broadcast_to(record, (8, EXTENT))
        pair_law[face, 2] = jnp.broadcast_to(scale, (8, EXTENT))

    for index in range(group):
        join_laws(near_base + index, near_law)
    for index in range(group):
        join_laws(far_base + index, far_law)

    def tall(tile):
        return jnp.concatenate([tile] * (times // 8), axis=0)

    for iteration in range(ITERS):
        half = halves[iteration]
        ascent_buffer = ascents[iteration]
        send_half(iteration, 0, faces).wait_recv()

        def linear(face):
            total = None
            for pair in range(stored // 2):
                left = half[columns[face, 0, 2 * pair]]
                right = half[columns[face, 0, 2 * pair + 1]]
                piece = jnp.concatenate([left, right], axis=1)
                block = jnp.concatenate([compliance[face, 2 * pair], compliance[face, 2 * pair + 1]], axis=0)
                product = jnp.dot(piece, block, preferred_element_type=jnp.float32)
                total = product if total is None else total + product
            ascent_buffer[face] = offset[face] - 2.0 * total

        for start in range(0, group, CHUNK):
            for index in range(start, start + CHUNK):
                linear(far_base + index)
            send_far(iteration, start, CHUNK).start()
        for index in range(group):
            linear(near_base + index)
        send_near(iteration, 0, group).start()

        def local(face, mates):
            index = jnp.maximum(partners[0, face], 0)
            turn = jnp.broadcast_to(orientation[face], (times, EXTENT))
            rigidity = tall(pair_law[face, 0])
            record = tall(pair_law[face, 1])
            scale = tall(pair_law[face, 2])
            mate = jnp.take_along_axis(mates[index], turn, axis=1)
            ascent = ascent_buffer[face]
            difference = ascent - mate
            peak = jnp.maximum(record, running_max(jnp.abs(difference * scale)))
            effective = rigidity * jnp.clip(FAILURE * SPAN - peak, 0.0, 1.0)
            stress = effective * difference / (1.0 + 2.0 * effective)
            if iteration == ITERS - 1:
                ascent_out[:, lanes(face)] = ascent
                traction_out[:, lanes(face)] = stress
            else:
                total = stress + (stress - ascent)
                offset[face] = total - 2.0 * load[:, lanes(face)].astype(jnp.float32)
                halves[iteration + 1][base + face] = total.astype(jnp.bfloat16)

        send_near(iteration, 0, group).wait_recv()
        for start in range(0, group, CHUNK):
            for index in range(start, start + CHUNK):
                local(near_base + index, nears[iteration])
            if iteration < ITERS - 1:
                send_half(iteration + 1, near_base + start, CHUNK).start()
        send_far(iteration, 0, group).wait_recv()
        for start in range(0, group, CHUNK):
            for index in range(start, start + CHUNK):
                local(far_base + index, fars[iteration])
            if iteration < ITERS - 1:
                send_half(iteration + 1, far_base + start, CHUNK).start()

    near_law_copy.wait_send()
    far_law_copy.wait_send()
    for iteration in range(ITERS):
        send_half(iteration, 0, faces).wait_send()
        send_near(iteration, 0, group).wait_send()
        send_far(iteration, 0, group).wait_send()


def shards(
    compliance,
    block_columns,
    load_response,
    starting_motion,
    start_traction,
    stiffness,
    history,
    face_partner,
    orientation,
):
    faces, stored = block_columns.shape[1:]
    times, width = starting_motion.shape[1:]
    group = faces // 2
    rows = lax.axis_size("row")
    vmem = pl.BlockSpec(memory_space=pltpu.VMEM)
    hbm = pl.BlockSpec(memory_space=pltpu.HBM)
    bf16 = jnp.bfloat16
    f32 = jnp.float32
    dma = pltpu.SemaphoreType.DMA
    scratch = (
        [
            pltpu.VMEM((faces, stored, EXTENT, EXTENT), bf16),
            pltpu.VMEM((times, width), bf16),
            pltpu.VMEM((times, width), bf16),
            pltpu.VMEM((times, width), bf16),
            pltpu.SMEM((faces, 1, stored), jnp.int32),
            pltpu.SMEM((1, faces), jnp.int32),
            pltpu.VMEM((1, width), f32),
            pltpu.VMEM((1, width), f32),
            pltpu.VMEM((faces, 1, EXTENT), jnp.int32),
            pltpu.VMEM((faces, times, EXTENT), f32),
            pltpu.VMEM((faces, 8, EXTENT), f32),
            pltpu.VMEM((group, 8, EXTENT), f32),
            pltpu.VMEM((group, 8, EXTENT), f32),
            pltpu.VMEM((faces, 3, 8, EXTENT), f32),
        ]
        + [pltpu.VMEM((rows * faces, times, EXTENT), bf16)] * ITERS
        + [pltpu.VMEM((faces, times, EXTENT), f32)] * ITERS
        + [pltpu.VMEM((group, times, EXTENT), f32)] * (2 * ITERS)
        + [dma((faces,)), dma((8,)), dma((2,)), dma((2,))]
        + [dma((ITERS,))] * 6
    )
    def keep(array):
        return pltpu.with_memory_space_constraint(array, pltpu.HBM)

    ascent, traction = pl.pallas_call(
        kernel,
        out_shape=[jax.ShapeDtypeStruct((times, width), f32)] * 2,
        in_specs=[hbm] * 9,
        out_specs=[vmem, vmem],
        scratch_shapes=scratch,
        compiler_params=pltpu.CompilerParams(
            collective_id=0, has_side_effects=True, vmem_limit_bytes=20 << 20
        ),
        name="latin",
    )(
        keep(jnp.transpose(block_columns, (1, 0, 2))),
        keep(face_partner),
        keep(compliance[0]),
        keep(load_response[0]),
        keep(starting_motion[0]),
        keep(start_traction[0]),
        keep(stiffness),
        keep(history),
        keep(jnp.transpose(orientation, (1, 0, 2))),
    )
    return (traction - ascent).astype(bf16)[None], traction.astype(bf16)[None]


def solution(mesh):
    in_specs = (
        P("sub", "row", None, None, None),
        P("sub", "row", None),
        P("sub", None, "row"),
        P("sub", None, "row"),
        P("sub", None, "row"),
        P("sub", "row"),
        P("sub", "row"),
        P("sub", "row"),
        P("sub", "row", None),
    )
    out_specs = (P("sub", None, "row"), P("sub", None, "row"))
    return jax.shard_map(shards, mesh=mesh, in_specs=in_specs, out_specs=out_specs, check_vma=False)
```

```python
import jax
import jax.numpy as jnp
from jax import lax
from jax.experimental import pallas as pl
from jax.experimental.pallas import tpu as pltpu
from jax.sharding import PartitionSpec as P

EXTENT = 128
ITERS = 3
ONSET = 0.15
FAILURE = 1.5
SPAN = 1.0 / (FAILURE - ONSET)
CHUNK = 3
COLUMN = 16
MESH = pl.DeviceIdType.MESH


def running_max(values):
    times = values.shape[0]
    step = 1
    while step < times:
        fill = jnp.zeros((step, values.shape[1]), values.dtype)
        values = jnp.maximum(values, jnp.concatenate([fill, values[: times - step]], axis=0))
        step *= 2
    return values


def kernel(
    columns_hbm,
    partners_hbm,
    compliance_hbm,
    load_hbm,
    motion_hbm,
    traction_hbm,
    stiffness_hbm,
    history_hbm,
    orientation_hbm,
    ascent_out,
    traction_out,
    compliance,
    load,
    motion,
    traction,
    columns,
    partners,
    stiffness,
    history,
    orientation,
    offset,
    own_law,
    near_law,
    far_law,
    pair_law,
    *scratch,
):
    halves = scratch[0:3]
    ascents = scratch[3:6]
    nears = scratch[6:9]
    fars = scratch[9:12]
    (block_sem, input_sem, law_send, law_recv, row_send, row_recv, near_send, near_recv, far_send, far_recv) = scratch[12:]

    faces, stored = compliance.shape[:2]
    times = motion.shape[0]
    group = faces // 2
    subs = lax.axis_size("sub")
    sub = lax.axis_index("sub")
    row = lax.axis_index("row")
    odd = lax.rem(sub, 2)
    near = {"sub": sub + 1 - 2 * odd}
    end = jnp.logical_or(sub == 0, sub == subs - 1)
    far = {"sub": jnp.where(end, sub, sub + 2 * odd - 1), "row": jnp.where(end, 1 - row, row)}
    mirror = {"row": 1 - row}
    near_base = group * odd
    far_base = group * (1 - odd)
    base = row * faces

    def lanes(face):
        if isinstance(face, int):
            return pl.ds(face * EXTENT, EXTENT)
        return pl.ds(pl.multiple_of(face * EXTENT, EXTENT), EXTENT)

    def fetch(source, target, index):
        return pltpu.make_async_copy(source, target, input_sem.at[index])

    def block_copy(face):
        return pltpu.make_async_copy(compliance_hbm.at[face], compliance.at[face], block_sem.at[face])

    def push(source, target, send, recv, device):
        return pltpu.make_async_remote_copy(
            src_ref=source, dst_ref=target, send_sem=send, recv_sem=recv, device_id=device, device_id_type=MESH
        )

    motion_copy = fetch(motion_hbm, motion, 0)
    traction_copy = fetch(traction_hbm, traction, 1)
    stiffness_copy = fetch(stiffness_hbm, stiffness, 2)
    history_copy = fetch(history_hbm, history, 3)
    load_copy = fetch(load_hbm, load, 4)
    columns_copy = fetch(columns_hbm, columns, 5)
    partners_copy = fetch(partners_hbm, partners, 6)
    orientation_copy = fetch(orientation_hbm, orientation, 7)
    motion_copy.start()
    traction_copy.start()

    place = lax.rem(sub, COLUMN)
    inner = jnp.logical_not(end)
    leads = jnp.logical_and(inner, place == 0)
    answers = jnp.logical_and(inner, place == COLUMN - 1)

    def greet(device):
        pl.semaphore_signal(barrier, inc=1, device_id=device, device_id_type=MESH)

    barrier = pltpu.get_barrier_semaphore()
    greet(mirror)
    greet(near)

    @pl.when(jnp.logical_not(jnp.logical_or(leads, answers)))
    def _():
        greet(far)

    stiffness_copy.start()
    history_copy.start()
    load_copy.start()
    for face in range(faces):
        block_copy(face).start()
    for copy in (columns_copy, partners_copy, orientation_copy):
        copy.start()

    def send_half(iteration, start, count):
        part = halves[iteration].at[pl.ds(base + start, count)]
        return push(part, part, row_send.at[iteration], row_recv.at[iteration], mirror)

    def send_near(iteration, start, count):
        return push(
            ascents[iteration].at[pl.ds(near_base + start, count)],
            nears[iteration].at[pl.ds(start, count)],
            near_send.at[iteration],
            near_recv.at[iteration],
            near,
        )

    def send_far(iteration, start, count):
        return push(
            ascents[iteration].at[pl.ds(far_base + start, count)],
            fars[iteration].at[pl.ds(start, count)],
            far_send.at[iteration],
            far_recv.at[iteration],
            far,
        )

    near_law_copy = push(own_law.at[pl.ds(near_base, group)], near_law, law_send.at[0], law_recv.at[0], near)
    far_law_copy = push(own_law.at[pl.ds(far_base, group)], far_law, law_send.at[1], law_recv.at[1], far)

    motion_copy.wait()
    traction_copy.wait()
    for face in range(faces):
        total = traction[:, lanes(face)].astype(jnp.float32) + motion[:, lanes(face)].astype(jnp.float32)
        offset[face] = total
        halves[0][base + face] = total.astype(jnp.bfloat16)

    pl.semaphore_wait(barrier, 3 - leads.astype(jnp.int32))
    send_half(0, 0, faces).start()

    @pl.when(jnp.logical_or(leads, answers))
    def _():
        greet(far)

    stiffness_copy.wait()
    history_copy.wait()
    for face in range(faces):
        own_law[face, 0:4] = jnp.broadcast_to(stiffness[0:1, lanes(face)], (4, EXTENT))
        own_law[face, 4:8] = jnp.broadcast_to(history[0:1, lanes(face)], (4, EXTENT))
    near_law_copy.start()

    @pl.when(jnp.logical_not(leads))
    def _():
        far_law_copy.start()

    load_copy.wait()
    for face in range(faces):
        offset[face] = offset[face] - 2.0 * load[:, lanes(face)].astype(jnp.float32)

    def turn_blocks(face, carry):
        block_copy(face).wait()
        for slot in range(stored):
            compliance[face, slot] = compliance[face, slot].T
        return carry

    lax.fori_loop(0, faces, turn_blocks, 0)

    for copy in (columns_copy, partners_copy, orientation_copy):
        copy.wait()
    near_law_copy.wait_recv()

    def join_laws(face, mate_laws):
        partner = partners[0, face]
        turn = jnp.broadcast_to(orientation[face], (8, EXTENT))
        mate = jnp.take_along_axis(mate_laws[jnp.maximum(partner, 0)], turn, axis=1)
        own = own_law[face]
        live = jnp.full((1, EXTENT), partner, jnp.int32) >= 0
        rigidity = jnp.where(live, 0.5 * (own[0:1] + mate[0:1]), 0.0)
        record = SPAN * jnp.maximum(own[4:5], mate[4:5])
        scale = SPAN / (1.0 + 2.0 * rigidity)
        pair_law[face, 0] = jnp.broadcast_to(rigidity, (8, EXTENT))
        pair_law[face, 1] = jnp.broadcast_to(record, (8, EXTENT))
        pair_law[face, 2] = jnp.broadcast_to(scale, (8, EXTENT))

    for index in range(group):
        join_laws(near_base + index, near_law)

    def tall(tile):
        return jnp.concatenate([tile] * (times // 8), axis=0)

    for iteration in range(ITERS):
        half = halves[iteration]
        ascent_buffer = ascents[iteration]
        send_half(iteration, 0, faces).wait_recv()

        def linear(face):
            total = None
            for pair in range(stored // 2):
                left = half[columns[face, 0, 2 * pair]]
                right = half[columns[face, 0, 2 * pair + 1]]
                piece = jnp.concatenate([left, right], axis=1)
                block = jnp.concatenate([compliance[face, 2 * pair], compliance[face, 2 * pair + 1]], axis=0)
                product = jnp.dot(piece, block, preferred_element_type=jnp.float32)
                total = product if total is None else total + product
            ascent_buffer[face] = offset[face] - 2.0 * total

        for start in range(0, group, CHUNK):
            for index in range(start, start + CHUNK):
                linear(far_base + index)
            if iteration == 0 and start == 0:

                @pl.when(leads)
                def _():
                    pl.semaphore_wait(barrier, 1)
                    far_law_copy.start()

            send_far(iteration, start, CHUNK).start()
        for index in range(group):
            linear(near_base + index)
        send_near(iteration, 0, group).start()

        def local(face, mates):
            index = jnp.maximum(partners[0, face], 0)
            turn = jnp.broadcast_to(orientation[face], (times, EXTENT))
            rigidity = tall(pair_law[face, 0])
            record = tall(pair_law[face, 1])
            scale = tall(pair_law[face, 2])
            mate = jnp.take_along_axis(mates[index], turn, axis=1)
            ascent = ascent_buffer[face]
            difference = ascent - mate
            peak = jnp.maximum(record, running_max(jnp.abs(difference * scale)))
            effective = rigidity * jnp.clip(FAILURE * SPAN - peak, 0.0, 1.0)
            stress = effective * difference / (1.0 + 2.0 * effective)
            if iteration == ITERS - 1:
                ascent_out[:, lanes(face)] = ascent
                traction_out[:, lanes(face)] = stress
            else:
                total = stress + (stress - ascent)
                offset[face] = total - 2.0 * load[:, lanes(face)].astype(jnp.float32)
                halves[iteration + 1][base + face] = total.astype(jnp.bfloat16)

        send_near(iteration, 0, group).wait_recv()
        for start in range(0, group, CHUNK):
            for index in range(start, start + CHUNK):
                local(near_base + index, nears[iteration])
            if iteration < ITERS - 1:
                send_half(iteration + 1, near_base + start, CHUNK).start()
        if iteration == 0:
            far_law_copy.wait_recv()
            for index in range(group):
                join_laws(far_base + index, far_law)
        send_far(iteration, 0, group).wait_recv()
        for start in range(0, group, CHUNK):
            for index in range(start, start + CHUNK):
                local(far_base + index, fars[iteration])
            if iteration < ITERS - 1:
                send_half(iteration + 1, far_base + start, CHUNK).start()

    near_law_copy.wait_send()
    far_law_copy.wait_send()
    for iteration in range(ITERS):
        send_half(iteration, 0, faces).wait_send()
        send_near(iteration, 0, group).wait_send()
        send_far(iteration, 0, group).wait_send()


def shards(
    compliance,
    block_columns,
    load_response,
    starting_motion,
    start_traction,
    stiffness,
    history,
    face_partner,
    orientation,
):
    faces, stored = block_columns.shape[1:]
    times, width = starting_motion.shape[1:]
    group = faces // 2
    rows = lax.axis_size("row")
    vmem = pl.BlockSpec(memory_space=pltpu.VMEM)
    hbm = pl.BlockSpec(memory_space=pltpu.HBM)
    bf16 = jnp.bfloat16
    f32 = jnp.float32
    dma = pltpu.SemaphoreType.DMA
    scratch = (
        [
            pltpu.VMEM((faces, stored, EXTENT, EXTENT), bf16),
            pltpu.VMEM((times, width), bf16),
            pltpu.VMEM((times, width), bf16),
            pltpu.VMEM((times, width), bf16),
            pltpu.SMEM((faces, 1, stored), jnp.int32),
            pltpu.SMEM((1, faces), jnp.int32),
            pltpu.VMEM((1, width), f32),
            pltpu.VMEM((1, width), f32),
            pltpu.VMEM((faces, 1, EXTENT), jnp.int32),
            pltpu.VMEM((faces, times, EXTENT), f32),
            pltpu.VMEM((faces, 8, EXTENT), f32),
            pltpu.VMEM((group, 8, EXTENT), f32),
            pltpu.VMEM((group, 8, EXTENT), f32),
            pltpu.VMEM((faces, 3, 8, EXTENT), f32),
        ]
        + [pltpu.VMEM((rows * faces, times, EXTENT), bf16)] * ITERS
        + [pltpu.VMEM((faces, times, EXTENT), f32)] * ITERS
        + [pltpu.VMEM((group, times, EXTENT), f32)] * (2 * ITERS)
        + [dma((faces,)), dma((8,)), dma((2,)), dma((2,))]
        + [dma((ITERS,))] * 6
    )
    def keep(array):
        return pltpu.with_memory_space_constraint(array, pltpu.HBM)

    ascent, traction = pl.pallas_call(
        kernel,
        out_shape=[jax.ShapeDtypeStruct((times, width), f32)] * 2,
        in_specs=[hbm] * 9,
        out_specs=[vmem, vmem],
        scratch_shapes=scratch,
        compiler_params=pltpu.CompilerParams(
            collective_id=0, has_side_effects=True, vmem_limit_bytes=20 << 20
        ),
        name="latin",
    )(
        keep(jnp.transpose(block_columns, (1, 0, 2))),
        keep(face_partner),
        keep(compliance[0]),
        keep(load_response[0]),
        keep(starting_motion[0]),
        keep(start_traction[0]),
        keep(stiffness),
        keep(history),
        keep(jnp.transpose(orientation, (1, 0, 2))),
    )
    return (traction - ascent).astype(bf16)[None], traction.astype(bf16)[None]


def solution(mesh):
    in_specs = (
        P("sub", "row", None, None, None),
        P("sub", "row", None),
        P("sub", None, "row"),
        P("sub", None, "row"),
        P("sub", None, "row"),
        P("sub", "row"),
        P("sub", "row"),
        P("sub", "row"),
        P("sub", "row", None),
    )
    out_specs = (P("sub", None, "row"), P("sub", None, "row"))
    return jax.shard_map(shards, mesh=mesh, in_specs=in_specs, out_specs=out_specs, check_vma=False)
```

```python
import jax
import jax.numpy as jnp
from jax import lax
from jax.experimental import pallas as pl
from jax.experimental.pallas import tpu as pltpu
from jax.sharding import PartitionSpec as P

EXTENT = 128
ITERS = 3
ONSET = 0.15
FAILURE = 1.5
SPAN = 1.0 / (FAILURE - ONSET)
CHUNK = 3
COLUMN = 16
MESH = pl.DeviceIdType.MESH


def running_max(values):
    times = values.shape[0]
    step = 1
    while step < times:
        fill = jnp.zeros((step, values.shape[1]), values.dtype)
        values = jnp.maximum(values, jnp.concatenate([fill, values[: times - step]], axis=0))
        step *= 2
    return values


def kernel(
    columns_hbm,
    partners_hbm,
    compliance_hbm,
    load_hbm,
    motion_hbm,
    traction_hbm,
    stiffness_hbm,
    history_hbm,
    orientation_hbm,
    ascent_out,
    traction_out,
    compliance,
    load,
    motion,
    traction,
    columns,
    partners,
    stiffness,
    history,
    orientation,
    offset,
    own_law,
    near_law,
    far_law,
    pair_law,
    *scratch,
):
    halves = scratch[0:3]
    ascents = scratch[3:6]
    nears = scratch[6:9]
    fars = scratch[9:12]
    (block_sem, input_sem, law_send, law_recv, row_send, row_recv, near_send, near_recv, far_send, far_recv) = scratch[12:]

    faces, stored = compliance.shape[:2]
    times = motion.shape[0]
    group = faces // 2
    subs = lax.axis_size("sub")
    sub = lax.axis_index("sub")
    row = lax.axis_index("row")
    odd = lax.rem(sub, 2)
    near = {"sub": sub + 1 - 2 * odd}
    end = jnp.logical_or(sub == 0, sub == subs - 1)
    far = {"sub": jnp.where(end, sub, sub + 2 * odd - 1), "row": jnp.where(end, 1 - row, row)}
    mirror = {"row": 1 - row}
    near_base = group * odd
    far_base = group * (1 - odd)
    base = row * faces

    def lanes(face):
        if isinstance(face, int):
            return pl.ds(face * EXTENT, EXTENT)
        return pl.ds(pl.multiple_of(face * EXTENT, EXTENT), EXTENT)

    def fetch(source, target, index):
        return pltpu.make_async_copy(source, target, input_sem.at[index])

    def block_copy(face):
        return pltpu.make_async_copy(compliance_hbm.at[face], compliance.at[face], block_sem.at[face])

    def push(source, target, send, recv, device):
        return pltpu.make_async_remote_copy(
            src_ref=source, dst_ref=target, send_sem=send, recv_sem=recv, device_id=device, device_id_type=MESH
        )

    motion_copy = fetch(motion_hbm, motion, 0)
    traction_copy = fetch(traction_hbm, traction, 1)
    stiffness_copy = fetch(stiffness_hbm, stiffness, 2)
    history_copy = fetch(history_hbm, history, 3)
    load_copy = fetch(load_hbm, load, 4)
    columns_copy = fetch(columns_hbm, columns, 5)
    partners_copy = fetch(partners_hbm, partners, 6)
    orientation_copy = fetch(orientation_hbm, orientation, 7)
    motion_copy.start()
    traction_copy.start()

    place = lax.rem(sub, COLUMN)
    inner = jnp.logical_not(end)
    leads = jnp.logical_and(inner, place == 0)
    answers = jnp.logical_and(inner, place == COLUMN - 1)

    def greet(device):
        pl.semaphore_signal(barrier, inc=1, device_id=device, device_id_type=MESH)

    barrier = pltpu.get_barrier_semaphore()
    greet(mirror)
    greet(near)

    @pl.when(jnp.logical_not(jnp.logical_or(leads, answers)))
    def _():
        greet(far)

    stiffness_copy.start()
    history_copy.start()
    load_copy.start()
    for face in range(group):
        block_copy(face).start()
    for copy in (columns_copy, partners_copy, orientation_copy):
        copy.start()

    def send_half(iteration, start, count):
        part = halves[iteration].at[pl.ds(base + start, count)]
        return push(part, part, row_send.at[iteration], row_recv.at[iteration], mirror)

    def send_near(iteration, start, count):
        return push(
            ascents[iteration].at[pl.ds(near_base + start, count)],
            nears[iteration].at[pl.ds(start, count)],
            near_send.at[iteration],
            near_recv.at[iteration],
            near,
        )

    def send_far(iteration, start, count):
        return push(
            ascents[iteration].at[pl.ds(far_base + start, count)],
            fars[iteration].at[pl.ds(start, count)],
            far_send.at[iteration],
            far_recv.at[iteration],
            far,
        )

    near_law_copy = push(own_law.at[pl.ds(near_base, group)], near_law, law_send.at[0], law_recv.at[0], near)
    far_law_copy = push(own_law.at[pl.ds(far_base, group)], far_law, law_send.at[1], law_recv.at[1], far)

    motion_copy.wait()
    traction_copy.wait()
    for face in range(faces):
        total = traction[:, lanes(face)].astype(jnp.float32) + motion[:, lanes(face)].astype(jnp.float32)
        offset[face] = total
        halves[0][base + face] = total.astype(jnp.bfloat16)

    pl.semaphore_wait(barrier, 3 - leads.astype(jnp.int32))
    send_half(0, 0, faces).start()
    for face in range(group, faces):
        block_copy(face).start()

    @pl.when(jnp.logical_or(leads, answers))
    def _():
        greet(far)

    stiffness_copy.wait()
    history_copy.wait()
    for face in range(faces):
        own_law[face, 0:4] = jnp.broadcast_to(stiffness[0:1, lanes(face)], (4, EXTENT))
        own_law[face, 4:8] = jnp.broadcast_to(history[0:1, lanes(face)], (4, EXTENT))
    near_law_copy.start()

    @pl.when(jnp.logical_not(leads))
    def _():
        far_law_copy.start()

    load_copy.wait()
    for face in range(faces):
        offset[face] = offset[face] - 2.0 * load[:, lanes(face)].astype(jnp.float32)

    def turn_blocks(face, carry):
        block_copy(face).wait()
        for slot in range(stored):
            compliance[face, slot] = compliance[face, slot].T
        return carry

    lax.fori_loop(0, faces, turn_blocks, 0)

    for copy in (columns_copy, partners_copy, orientation_copy):
        copy.wait()
    near_law_copy.wait_recv()

    def join_laws(face, mate_laws):
        partner = partners[0, face]
        turn = jnp.broadcast_to(orientation[face], (8, EXTENT))
        mate = jnp.take_along_axis(mate_laws[jnp.maximum(partner, 0)], turn, axis=1)
        own = own_law[face]
        live = jnp.full((1, EXTENT), partner, jnp.int32) >= 0
        rigidity = jnp.where(live, 0.5 * (own[0:1] + mate[0:1]), 0.0)
        record = SPAN * jnp.maximum(own[4:5], mate[4:5])
        scale = SPAN / (1.0 + 2.0 * rigidity)
        pair_law[face, 0] = jnp.broadcast_to(rigidity, (8, EXTENT))
        pair_law[face, 1] = jnp.broadcast_to(record, (8, EXTENT))
        pair_law[face, 2] = jnp.broadcast_to(scale, (8, EXTENT))

    for index in range(group):
        join_laws(near_base + index, near_law)

    def tall(tile):
        return jnp.concatenate([tile] * (times // 8), axis=0)

    for iteration in range(ITERS):
        half = halves[iteration]
        ascent_buffer = ascents[iteration]
        send_half(iteration, 0, faces).wait_recv()

        def linear(face):
            total = None
            for pair in range(stored // 2):
                left = half[columns[face, 0, 2 * pair]]
                right = half[columns[face, 0, 2 * pair + 1]]
                piece = jnp.concatenate([left, right], axis=1)
                block = jnp.concatenate([compliance[face, 2 * pair], compliance[face, 2 * pair + 1]], axis=0)
                product = jnp.dot(piece, block, preferred_element_type=jnp.float32)
                total = product if total is None else total + product
            ascent_buffer[face] = offset[face] - 2.0 * total

        for start in range(0, group, CHUNK):
            for index in range(start, start + CHUNK):
                linear(far_base + index)
            if iteration == 0 and start == 0:

                @pl.when(leads)
                def _():
                    pl.semaphore_wait(barrier, 1)
                    far_law_copy.start()

            send_far(iteration, start, CHUNK).start()
        for index in range(group):
            linear(near_base + index)
        send_near(iteration, 0, group).start()

        def local(face, mates):
            index = jnp.maximum(partners[0, face], 0)
            turn = jnp.broadcast_to(orientation[face], (times, EXTENT))
            rigidity = tall(pair_law[face, 0])
            record = tall(pair_law[face, 1])
            scale = tall(pair_law[face, 2])
            mate = jnp.take_along_axis(mates[index], turn, axis=1)
            ascent = ascent_buffer[face]
            difference = ascent - mate
            peak = jnp.maximum(record, running_max(jnp.abs(difference * scale)))
            effective = rigidity * jnp.clip(FAILURE * SPAN - peak, 0.0, 1.0)
            stress = effective * difference / (1.0 + 2.0 * effective)
            if iteration == ITERS - 1:
                ascent_out[:, lanes(face)] = ascent
                traction_out[:, lanes(face)] = stress
            else:
                total = stress + (stress - ascent)
                offset[face] = total - 2.0 * load[:, lanes(face)].astype(jnp.float32)
                halves[iteration + 1][base + face] = total.astype(jnp.bfloat16)

        send_near(iteration, 0, group).wait_recv()
        for start in range(0, group, CHUNK):
            for index in range(start, start + CHUNK):
                local(near_base + index, nears[iteration])
            if iteration < ITERS - 1:
                send_half(iteration + 1, near_base + start, CHUNK).start()
        if iteration == 0:
            far_law_copy.wait_recv()
            for index in range(group):
                join_laws(far_base + index, far_law)
        send_far(iteration, 0, group).wait_recv()
        start = 0
        for count in (1, 2, 3, 3):
            for index in range(start, start + count):
                local(far_base + index, fars[iteration])
            if iteration < ITERS - 1:
                send_half(iteration + 1, far_base + start, count).start()
            start += count

    near_law_copy.wait_send()
    far_law_copy.wait_send()
    for iteration in range(ITERS):
        send_half(iteration, 0, faces).wait_send()
        send_near(iteration, 0, group).wait_send()
        send_far(iteration, 0, group).wait_send()


def shards(
    compliance,
    block_columns,
    load_response,
    starting_motion,
    start_traction,
    stiffness,
    history,
    face_partner,
    orientation,
):
    faces, stored = block_columns.shape[1:]
    times, width = starting_motion.shape[1:]
    group = faces // 2
    rows = lax.axis_size("row")
    vmem = pl.BlockSpec(memory_space=pltpu.VMEM)
    hbm = pl.BlockSpec(memory_space=pltpu.HBM)
    bf16 = jnp.bfloat16
    f32 = jnp.float32
    dma = pltpu.SemaphoreType.DMA
    scratch = (
        [
            pltpu.VMEM((faces, stored, EXTENT, EXTENT), bf16),
            pltpu.VMEM((times, width), bf16),
            pltpu.VMEM((times, width), bf16),
            pltpu.VMEM((times, width), bf16),
            pltpu.SMEM((faces, 1, stored), jnp.int32),
            pltpu.SMEM((1, faces), jnp.int32),
            pltpu.VMEM((1, width), f32),
            pltpu.VMEM((1, width), f32),
            pltpu.VMEM((faces, 1, EXTENT), jnp.int32),
            pltpu.VMEM((faces, times, EXTENT), f32),
            pltpu.VMEM((faces, 8, EXTENT), f32),
            pltpu.VMEM((group, 8, EXTENT), f32),
            pltpu.VMEM((group, 8, EXTENT), f32),
            pltpu.VMEM((faces, 3, 8, EXTENT), f32),
        ]
        + [pltpu.VMEM((rows * faces, times, EXTENT), bf16)] * ITERS
        + [pltpu.VMEM((faces, times, EXTENT), f32)] * ITERS
        + [pltpu.VMEM((group, times, EXTENT), f32)] * (2 * ITERS)
        + [dma((faces,)), dma((8,)), dma((2,)), dma((2,))]
        + [dma((ITERS,))] * 6
    )
    def keep(array):
        return pltpu.with_memory_space_constraint(array, pltpu.HBM)

    ascent, traction = pl.pallas_call(
        kernel,
        out_shape=[jax.ShapeDtypeStruct((times, width), f32)] * 2,
        in_specs=[hbm] * 9,
        out_specs=[vmem, vmem],
        scratch_shapes=scratch,
        compiler_params=pltpu.CompilerParams(
            collective_id=0, has_side_effects=True, vmem_limit_bytes=20 << 20,
        ),
        name="latin",
    )(
        keep(jnp.transpose(block_columns, (1, 0, 2))),
        keep(face_partner),
        keep(compliance[0]),
        keep(load_response[0]),
        keep(starting_motion[0]),
        keep(start_traction[0]),
        keep(stiffness),
        keep(history),
        keep(jnp.transpose(orientation, (1, 0, 2))),
    )
    return (traction - ascent).astype(bf16)[None], traction.astype(bf16)[None]


def solution(mesh):
    in_specs = (
        P("sub", "row", None, None, None),
        P("sub", "row", None),
        P("sub", None, "row"),
        P("sub", None, "row"),
        P("sub", None, "row"),
        P("sub", "row"),
        P("sub", "row"),
        P("sub", "row"),
        P("sub", "row", None),
    )
    out_specs = (P("sub", None, "row"), P("sub", None, "row"))
    return jax.shard_map(shards, mesh=mesh, in_specs=in_specs, out_specs=out_specs, check_vma=False)
```

```python
import jax
import jax.numpy as jnp
from jax import lax
from jax.experimental import pallas as pl
from jax.experimental.pallas import tpu as pltpu
from jax.sharding import PartitionSpec as P

EXTENT = 128
ITERS = 3
ONSET = 0.15
FAILURE = 1.5
SPAN = 1.0 / (FAILURE - ONSET)
CHUNK = 3
COLUMN = 16
MESH = pl.DeviceIdType.MESH


def running_max(values):
    times = values.shape[0]
    step = 1
    while step < times:
        fill = jnp.zeros((step, values.shape[1]), values.dtype)
        values = jnp.maximum(values, jnp.concatenate([fill, values[: times - step]], axis=0))
        step *= 2
    return values


def kernel(
    columns_hbm,
    partners_hbm,
    compliance_hbm,
    load_hbm,
    motion_hbm,
    traction_hbm,
    stiffness_hbm,
    history_hbm,
    orientation_hbm,
    ascent_out,
    traction_out,
    compliance,
    load,
    motion,
    traction,
    columns,
    partners,
    stiffness,
    history,
    orientation,
    offset,
    own_law,
    near_law,
    far_law,
    pair_law,
    *scratch,
):
    halves = scratch[0:3]
    ascents = scratch[3:6]
    nears = scratch[6:9]
    fars = scratch[9:12]
    (block_sem, input_sem, law_send, law_recv, row_send, row_recv, near_send, near_recv, far_send, far_recv) = scratch[12:]

    faces, stored = compliance.shape[:2]
    times = motion.shape[0]
    group = faces // 2
    subs = lax.axis_size("sub")
    sub = lax.axis_index("sub")
    row = lax.axis_index("row")
    odd = lax.rem(sub, 2)
    near = {"sub": sub + 1 - 2 * odd}
    end = jnp.logical_or(sub == 0, sub == subs - 1)
    far = {"sub": jnp.where(end, sub, sub + 2 * odd - 1), "row": jnp.where(end, 1 - row, row)}
    mirror = {"row": 1 - row}
    near_base = group * odd
    far_base = group * (1 - odd)
    base = row * faces

    def lanes(face):
        if isinstance(face, int):
            return pl.ds(face * EXTENT, EXTENT)
        return pl.ds(pl.multiple_of(face * EXTENT, EXTENT), EXTENT)

    def fetch(source, target, index):
        return pltpu.make_async_copy(source, target, input_sem.at[index])

    def block_copy(face):
        return pltpu.make_async_copy(compliance_hbm.at[face], compliance.at[face], block_sem.at[face])

    def push(source, target, send, recv, device):
        return pltpu.make_async_remote_copy(
            src_ref=source, dst_ref=target, send_sem=send, recv_sem=recv, device_id=device, device_id_type=MESH
        )

    motion_copy = fetch(motion_hbm, motion, 0)
    traction_copy = fetch(traction_hbm, traction, 1)
    stiffness_copy = fetch(stiffness_hbm, stiffness, 2)
    history_copy = fetch(history_hbm, history, 3)
    load_copy = fetch(load_hbm, load, 4)
    columns_copy = fetch(columns_hbm, columns, 5)
    partners_copy = fetch(partners_hbm, partners, 6)
    orientation_copy = fetch(orientation_hbm, orientation, 7)
    motion_copy.start()
    traction_copy.start()

    place = lax.rem(sub, COLUMN)
    inner = jnp.logical_not(end)
    leads = jnp.logical_and(inner, place == 0)
    answers = jnp.logical_and(inner, place == COLUMN - 1)

    def greet(device):
        pl.semaphore_signal(barrier, inc=1, device_id=device, device_id_type=MESH)

    barrier = pltpu.get_barrier_semaphore()
    greet(mirror)
    greet(near)

    @pl.when(jnp.logical_not(jnp.logical_or(leads, answers)))
    def _():
        greet(far)

    stiffness_copy.start()
    history_copy.start()
    load_copy.start()
    for face in range(group):
        block_copy(face).start()
    for copy in (columns_copy, partners_copy, orientation_copy):
        copy.start()

    def send_half(iteration, start, count):
        part = halves[iteration].at[pl.ds(base + start, count)]
        return push(part, part, row_send.at[iteration], row_recv.at[iteration], mirror)

    def send_near(iteration, start, count):
        return push(
            ascents[iteration].at[pl.ds(near_base + start, count)],
            nears[iteration].at[pl.ds(start, count)],
            near_send.at[iteration],
            near_recv.at[iteration],
            near,
        )

    def send_far(iteration, start, count):
        return push(
            ascents[iteration].at[pl.ds(far_base + start, count)],
            fars[iteration].at[pl.ds(start, count)],
            far_send.at[iteration],
            far_recv.at[iteration],
            far,
        )

    near_law_copy = push(own_law.at[pl.ds(near_base, group)], near_law, law_send.at[0], law_recv.at[0], near)
    far_law_copy = push(own_law.at[pl.ds(far_base, group)], far_law, law_send.at[1], law_recv.at[1], far)

    motion_copy.wait()
    traction_copy.wait()
    for face in range(faces):
        total = traction[:, lanes(face)].astype(jnp.float32) + motion[:, lanes(face)].astype(jnp.float32)
        offset[face] = total
        halves[0][base + face] = total.astype(jnp.bfloat16)

    pl.semaphore_wait(barrier, 3 - leads.astype(jnp.int32))
    send_half(0, 0, faces).start()
    for face in range(group, faces):
        block_copy(face).start()

    @pl.when(jnp.logical_or(leads, answers))
    def _():
        greet(far)

    stiffness_copy.wait()
    history_copy.wait()
    for face in range(faces):
        own_law[face, 0:4] = jnp.broadcast_to(stiffness[0:1, lanes(face)], (4, EXTENT))
        own_law[face, 4:8] = jnp.broadcast_to(history[0:1, lanes(face)], (4, EXTENT))
    near_law_copy.start()

    @pl.when(jnp.logical_not(leads))
    def _():
        far_law_copy.start()

    load_copy.wait()
    for face in range(faces):
        offset[face] = offset[face] - 2.0 * load[:, lanes(face)].astype(jnp.float32)

    def turn_blocks(face, carry):
        block_copy(face).wait()
        for slot in range(stored):
            compliance[face, slot] = compliance[face, slot].T
        return carry

    lax.fori_loop(0, faces, turn_blocks, 0)

    for copy in (columns_copy, partners_copy, orientation_copy):
        copy.wait()
    near_law_copy.wait_recv()

    def join_laws(face, mate_laws):
        partner = partners[0, face]
        turn = jnp.broadcast_to(orientation[face], (8, EXTENT))
        mate = jnp.take_along_axis(mate_laws[jnp.maximum(partner, 0)], turn, axis=1)
        own = own_law[face]
        live = jnp.full((1, EXTENT), partner, jnp.int32) >= 0
        rigidity = jnp.where(live, 0.5 * (own[0:1] + mate[0:1]), 0.0)
        record = SPAN * jnp.maximum(own[4:5], mate[4:5])
        scale = SPAN / (1.0 + 2.0 * rigidity)
        pair_law[face, 0] = jnp.broadcast_to(rigidity, (8, EXTENT))
        pair_law[face, 1] = jnp.broadcast_to(record, (8, EXTENT))
        pair_law[face, 2] = jnp.broadcast_to(scale, (8, EXTENT))

    for index in range(group):
        join_laws(near_base + index, near_law)

    def tall(tile):
        return jnp.concatenate([tile] * (times // 8), axis=0)

    for iteration in range(ITERS):
        half = halves[iteration]
        ascent_buffer = ascents[iteration]
        send_half(iteration, 0, faces).wait_recv()

        def linear(face):
            total = None
            for pair in range(stored // 2):
                left = half[columns[face, 0, 2 * pair]]
                right = half[columns[face, 0, 2 * pair + 1]]
                piece = jnp.concatenate([left, right], axis=1)
                block = jnp.concatenate([compliance[face, 2 * pair], compliance[face, 2 * pair + 1]], axis=0)
                product = jnp.dot(piece, block, preferred_element_type=jnp.float32)
                total = product if total is None else total + product
            ascent_buffer[face] = offset[face] - 2.0 * total

        for start in range(0, group, CHUNK):
            for index in range(start, start + CHUNK):
                linear(far_base + index)
            if iteration == 0 and start == 0:

                @pl.when(leads)
                def _():
                    pl.semaphore_wait(barrier, 1)
                    far_law_copy.start()

            send_far(iteration, start, CHUNK).start()
        for index in range(group):
            linear(near_base + index)
        send_near(iteration, 0, group).start()

        def local(face, mates):
            index = jnp.maximum(partners[0, face], 0)
            turn = jnp.broadcast_to(orientation[face], (times, EXTENT))
            rigidity = tall(pair_law[face, 0])
            record = tall(pair_law[face, 1])
            scale = tall(pair_law[face, 2])
            mate = jnp.take_along_axis(mates[index], turn, axis=1)
            ascent = ascent_buffer[face]
            difference = ascent - mate
            peak = jnp.maximum(record, running_max(jnp.abs(difference * scale)))
            effective = rigidity * jnp.clip(FAILURE * SPAN - peak, 0.0, 1.0)
            stress = effective * difference / (1.0 + 2.0 * effective)
            if iteration == ITERS - 1:
                ascent_out[:, lanes(face)] = ascent
                traction_out[:, lanes(face)] = stress
            else:
                total = stress + (stress - ascent)
                offset[face] = total - 2.0 * load[:, lanes(face)].astype(jnp.float32)
                halves[iteration + 1][base + face] = total.astype(jnp.bfloat16)

        if iteration == ITERS - 1:
            near_law_copy.wait_send()
            far_law_copy.wait_send()
            for earlier in range(ITERS):
                send_half(earlier, 0, faces).wait_send()
                if earlier < ITERS - 1:
                    send_near(earlier, 0, group).wait_send()
                    send_far(earlier, 0, group).wait_send()

        send_near(iteration, 0, group).wait_recv()
        for start in range(0, group, CHUNK):
            for index in range(start, start + CHUNK):
                local(near_base + index, nears[iteration])
            if iteration < ITERS - 1:
                send_half(iteration + 1, near_base + start, CHUNK).start()
        if iteration == 0:
            far_law_copy.wait_recv()
            for index in range(group):
                join_laws(far_base + index, far_law)
        send_far(iteration, 0, group).wait_recv()
        start = 0
        for count in (1, 2, 3, 3):
            for index in range(start, start + count):
                local(far_base + index, fars[iteration])
            if iteration < ITERS - 1:
                send_half(iteration + 1, far_base + start, count).start()
            start += count

    send_near(ITERS - 1, 0, group).wait_send()
    send_far(ITERS - 1, 0, group).wait_send()


def shards(
    compliance,
    block_columns,
    load_response,
    starting_motion,
    start_traction,
    stiffness,
    history,
    face_partner,
    orientation,
):
    faces, stored = block_columns.shape[1:]
    times, width = starting_motion.shape[1:]
    group = faces // 2
    rows = lax.axis_size("row")
    vmem = pl.BlockSpec(memory_space=pltpu.VMEM)
    hbm = pl.BlockSpec(memory_space=pltpu.HBM)
    bf16 = jnp.bfloat16
    f32 = jnp.float32
    dma = pltpu.SemaphoreType.DMA
    scratch = (
        [
            pltpu.VMEM((faces, stored, EXTENT, EXTENT), bf16),
            pltpu.VMEM((times, width), bf16),
            pltpu.VMEM((times, width), bf16),
            pltpu.VMEM((times, width), bf16),
            pltpu.SMEM((faces, 1, stored), jnp.int32),
            pltpu.SMEM((1, faces), jnp.int32),
            pltpu.VMEM((1, width), f32),
            pltpu.VMEM((1, width), f32),
            pltpu.VMEM((faces, 1, EXTENT), jnp.int32),
            pltpu.VMEM((faces, times, EXTENT), f32),
            pltpu.VMEM((faces, 8, EXTENT), f32),
            pltpu.VMEM((group, 8, EXTENT), f32),
            pltpu.VMEM((group, 8, EXTENT), f32),
            pltpu.VMEM((faces, 3, 8, EXTENT), f32),
        ]
        + [pltpu.VMEM((rows * faces, times, EXTENT), bf16)] * ITERS
        + [pltpu.VMEM((faces, times, EXTENT), f32)] * ITERS
        + [pltpu.VMEM((group, times, EXTENT), f32)] * (2 * ITERS)
        + [dma((faces,)), dma((8,)), dma((2,)), dma((2,))]
        + [dma((ITERS,))] * 6
    )
    def keep(array):
        return pltpu.with_memory_space_constraint(array, pltpu.HBM)

    ascent, traction = pl.pallas_call(
        kernel,
        out_shape=[jax.ShapeDtypeStruct((times, width), f32)] * 2,
        in_specs=[hbm] * 9,
        out_specs=[vmem, vmem],
        scratch_shapes=scratch,
        compiler_params=pltpu.CompilerParams(
            collective_id=0, has_side_effects=True, vmem_limit_bytes=20 << 20,
        ),
        name="latin",
    )(
        keep(jnp.transpose(block_columns, (1, 0, 2))),
        keep(face_partner),
        keep(compliance[0]),
        keep(load_response[0]),
        keep(starting_motion[0]),
        keep(start_traction[0]),
        keep(stiffness),
        keep(history),
        keep(jnp.transpose(orientation, (1, 0, 2))),
    )
    return (traction - ascent).astype(bf16)[None], traction.astype(bf16)[None]


def solution(mesh):
    in_specs = (
        P("sub", "row", None, None, None),
        P("sub", "row", None),
        P("sub", None, "row"),
        P("sub", None, "row"),
        P("sub", None, "row"),
        P("sub", "row"),
        P("sub", "row"),
        P("sub", "row"),
        P("sub", "row", None),
    )
    out_specs = (P("sub", None, "row"), P("sub", None, "row"))
    return jax.shard_map(shards, mesh=mesh, in_specs=in_specs, out_specs=out_specs, check_vma=False)
```
